32 devices in a mesh: view: 8 (over z, x), head: 4 (over y, core).
Axes of the slice: x: 2, y: 2, z: 4, core: 2. Of those that a mesh axis runs over, the one named last changes fastest.
Arguments:
- features: bfloat16 [16384, 1024], P(('view', 'head')), may hold values from -6 to 6
- attend_weight: bfloat16 [2, 3, 1024, 1024], P(None, None, 'view', 'head'), may hold values from -0.1875 to 0.1875
- output_weight: bfloat16 [2, 1024, 1024], P(None, 'view'), may hold values from -0.1875 to 0.1875
- fast_init: bfloat16 [2, 16, 3, 64, 512], P(None, 'head', None, None, 'view'), may hold values from -0.75 to 0.75
- update_mask: int32 [8, 2048], P('view'), may hold values 0 or 1
Outputs:
- refined: bfloat16 [16384, 1024], P(('view', 'head'))
The draws below stay inside these ranges and needn't reach their ends.
All inputs are finite; a program needn't handle non-finite values. No bound on the sum of `update_mask` on one device may be relied on, other than what follows from the above.
Results may differ from the reference program's by a relative error of at most 0.035.
Values may be sent and summed in bfloat16 or wider, within the bound.
No kernel may reach another device: no remote copies, remote signals or barrier semaphores. Data moves between devices by JAX's collectives and lax.ppermute only.
A program may use at most 64 MiB of HBM per device.

```python
import jax
import jax.numpy as jnp
from jax import lax

D = 1024
H = 16
DH = 64
FH = 512
VIEW_LEN = 2048
BLOCKS = 2
NS_STEPS = 5
VIEWS = 8
TOKENS = 16384


def plant(drawn, own_key, least, largest):
    extent = drawn.shape
    place = [jax.random.randint(jax.random.fold_in(own_key, axis), (), 0, extent[axis]) for axis in range(len(extent))]
    drawn = drawn.at[tuple(place)].set(least)
    longest = extent.index(max(extent))
    place[longest] = (place[longest] + 1) % extent[longest]
    return drawn.at[tuple(place)].set(largest)


def levels(stream_key, shape, shards, least, high):
    loudness, own = 1.0, jax.random.fold_in(stream_key, 6)
    for position, blocks in shards:
        draws = jnp.exp(jax.random.uniform(jax.random.fold_in(own, position), (blocks,), jnp.float32, least / len(shards), high / len(shards)))
        loudness = loudness * jnp.repeat(draws, shape[position] // blocks).reshape([-1 if axis == position else 1 for axis in range(len(shape))])
    return loudness


def gaussian(rng, shape, deviation, bound, pieces=(), dtype=jnp.bfloat16):
    result = deviation * jax.random.normal(rng, shape, jnp.float32)
    if pieces:
        result = result * levels(rng, shape, pieces, -0.22, 0.18)
    return jnp.clip(result, -bound, bound).astype(dtype)


def setup_inputs(seed: int = 0) -> dict:
    splits = jax.random.split(jax.random.key(seed), 6)
    features = gaussian(splits[0], (TOKENS, D), 1.0, 6.0, ((0, 32),))
    attend_weight = gaussian(splits[1], (BLOCKS, 3, D, D), D ** -0.5, 0.1875, ((2, 8), (3, 4)))
    output_weight = gaussian(splits[2], (BLOCKS, D, D), D ** -0.5, 0.1875, ((1, 8),))
    fast_init = gaussian(splits[3], (BLOCKS, H, 3, DH, FH), DH ** -0.5, 0.75, ((1, 4), (4, 8)))
    update_mask = plant((jax.random.randint(splits[4], (VIEWS, VIEW_LEN), 0, 4) < 3).astype(jnp.int32), jax.random.fold_in(splits[4], 1), 0, 1)
    return dict(features=features, attend_weight=attend_weight, output_weight=output_weight, fast_init=fast_init, update_mask=update_mask)


newton_coeffs = (3.4445, -4.775, 2.0315)
learn_rate = 1.0
score_scale = 0.25

def normalize(values, epsilon):
    return values * lax.rsqrt(lax.optimization_barrier(jnp.mean(values * values, axis=-1, keepdims=True)) + epsilon)

def newton_step(current, gram_matrix):
    squared = jnp.einsum('...de,...ef->...df', gram_matrix, gram_matrix, precision=lax.Precision.HIGHEST)
    polynomial = newton_coeffs[1] * gram_matrix + newton_coeffs[2] * squared
    return newton_coeffs[0] * current + jnp.einsum('...de,...ef->...df', polynomial, current, precision=lax.Precision.HIGHEST)

def orthogonalize(gradients):
    squares = lax.optimization_barrier(jnp.sum(gradients * gradients, axis=(-2, -1), keepdims=True))
    current = gradients * lax.rsqrt(squares + 1e-06)
    for _ in range(NS_STEPS):
        gram_matrix = jnp.einsum('...df,...ef->...de', current, current, precision=lax.Precision.HIGHEST)
        current = newton_step(current, gram_matrix)
    return current

def fast_gradient(keys, values, mask, weights):
    wide = weights.astype(jnp.float32)
    key_wide = keys.astype(jnp.float32)
    first = jnp.einsum('thd,hdf->thf', key_wide, wide[:, 0])
    third = jnp.einsum('thd,hdf->thf', key_wide, wide[:, 1])
    sigma = jax.nn.sigmoid(first)
    hidden = (first * sigma * third).astype(jnp.bfloat16)
    target = (-(mask[:, None, None].astype(jnp.float32) * values.astype(jnp.float32))).astype(jnp.bfloat16)
    back = jnp.einsum('thd,hdf->thf', target.astype(jnp.float32), wide[:, 2])
    d_third = (back * first * sigma).astype(jnp.bfloat16)
    d_first = (back * third * sigma * (1.0 + first * (1.0 - sigma))).astype(jnp.bfloat16)
    grad_first = jnp.einsum('thd,thf->hdf', key_wide, d_first.astype(jnp.float32))
    grad_third = jnp.einsum('thd,thf->hdf', key_wide, d_third.astype(jnp.float32))
    grad_last = jnp.einsum('thd,thf->hdf', target.astype(jnp.float32), hidden.astype(jnp.float32))
    return jnp.stack([grad_first, grad_third, grad_last], axis=1)

def fast_apply(queries, weights):
    wide = weights.astype(jnp.float32)
    query_wide = queries.astype(jnp.float32)
    first = jnp.einsum('thd,hdf->thf', query_wide, wide[:, 0])
    third = jnp.einsum('thd,hdf->thf', query_wide, wide[:, 1])
    hidden = (first * jax.nn.sigmoid(first) * third).astype(jnp.bfloat16)
    output = jnp.einsum('thf,hdf->thd', hidden.astype(jnp.float32), wide[:, 2])
    return normalize(output, 1e-05)

def attend(queries, keys, values):
    scores = jnp.einsum('qhd,khd->hqk', queries.astype(jnp.float32), keys.astype(jnp.float32)) * score_scale
    expo = jnp.exp(scores)
    probs = (expo / lax.optimization_barrier(jnp.sum(expo, axis=-1, keepdims=True))).astype(jnp.bfloat16)
    return jnp.einsum('hqk,khd->qhd', probs.astype(jnp.float32), values.astype(jnp.float32))

def reference(features, attend_weight, output_weight, fast_init, update_mask):
    stream = features
    for layer in range(BLOCKS):
        normed = normalize(stream.astype(jnp.float32), 1e-05).astype(jnp.bfloat16)
        packed = jnp.stack([jnp.dot(normed, attend_weight[layer, which], preferred_element_type=jnp.float32) for which in range(3)], axis=1).astype(jnp.bfloat16)
        packed = packed.reshape(VIEWS, VIEW_LEN, 3, H, DH)
        queries = normalize(packed[:, :, 0].astype(jnp.float32), 1e-05).astype(jnp.bfloat16)
        keys = normalize(packed[:, :, 1].astype(jnp.float32), 1e-05).astype(jnp.bfloat16)
        values = packed[:, :, 2]
        initial = fast_init[layer]

        def accumulate(total, inputs):
            return (total + fast_gradient(inputs[0], inputs[1], inputs[2], initial), None)
        gradients, _ = lax.scan(accumulate, jnp.zeros((H, 3, DH, FH), jnp.float32), (keys, values, update_mask))
        updated = (initial.astype(jnp.float32) - learn_rate * orthogonalize(gradients)).astype(jnp.bfloat16)

        def mix_view(inputs):
            return (attend(inputs[0], inputs[1], inputs[2]) + fast_apply(inputs[0], updated)).astype(jnp.bfloat16)
        mixed = lax.map(mix_view, (queries, keys, values)).reshape(TOKENS, D)
        projected = jnp.dot(mixed, output_weight[layer], preferred_element_type=jnp.float32)
        stream = (stream.astype(jnp.float32) + projected).astype(jnp.bfloat16)
    return stream
```

```python
import functools
import math

import jax
import jax.numpy as jnp
from jax import lax
from jax.experimental import pallas as pl
from jax.experimental.pallas import tpu as pltpu
from jax.sharding import PartitionSpec as P

BLOCKS = 2
NS_STEPS = 5

newton_coeffs = (3.4445, -4.775, 2.0315)
learn_rate = 1.0
score_scale = 0.25
log2_e = math.log2(math.e)

F32, BF16 = jnp.float32, jnp.bfloat16
SMEM = pl.BlockSpec(memory_space=pltpu.SMEM)


def mm(a, b, ca, cb, precision=None):
    return lax.dot_general(
        a, b, (((ca,), (cb,)), ((), ())), preferred_element_type=F32, precision=precision
    )


def whole(shape):
    return pl.BlockSpec(tuple(shape), lambda i: (0,) * len(shape))


def cost(flops, nbytes, trans=0):
    return pl.CostEstimate(flops=int(flops), bytes_accessed=int(nbytes), transcendentals=int(trans))


def sigmoid(x):
    return 0.5 * jnp.tanh(0.5 * x) + 0.5


def unit(part, axis):
    return part * lax.rsqrt(jnp.mean(part * part, axis=axis, keepdims=True) + 1e-05)


def prepare_kernel(count, d_slab, f_slab, heads, dim, ids_ref, *refs):
    slabs, (wt_ref, ft_ref), (w_all, f_all) = refs[:count], refs[count : count + 2], refs[count + 2 :]
    cols = heads * dim
    for k in range(count):
        source = ids_ref[0] ^ k
        for j in range(3):
            w_all[j, pl.ds(pl.multiple_of(source * d_slab, d_slab), d_slab)] = slabs[k][
                j * d_slab : (j + 1) * d_slab
            ]
            f_all[j, pl.ds(pl.multiple_of(source * f_slab, f_slab), f_slab)] = slabs[k][
                3 * d_slab + j * f_slab : 3 * d_slab + (j + 1) * f_slab
            ]
    for j in range(3):
        wt_ref[j * cols : (j + 1) * cols] = w_all[j].T
        for h in range(heads):
            ft_ref[h, j] = f_all[j, :, h * dim : (h + 1) * dim]


def prepare(ids, slabs, d_slab, f_slab, heads, dim):
    count = len(slabs)
    cols = heads * dim
    depth, units = count * d_slab, count * f_slab
    return pl.pallas_call(
        functools.partial(prepare_kernel, count, d_slab, f_slab, heads, dim),
        grid=(1,),
        in_specs=[SMEM] + [whole(s.shape) for s in slabs],
        out_specs=[whole((3 * cols, depth)), whole((heads, 3, units, dim))],
        out_shape=[
            jax.ShapeDtypeStruct((3 * cols, depth), BF16),
            jax.ShapeDtypeStruct((heads, 3, units, dim), BF16),
        ],
        scratch_shapes=[pltpu.VMEM((3, depth, cols), BF16), pltpu.VMEM((3, units, cols), BF16)],
        cost_estimate=cost(0, 8 * 2**20),
        name="prepare",
    )(ids, *slabs)


def front_kernel(heads, dim, chunks, steps, base, tokens, last, ids_ref, mask_ref, wt_ref, ft_ref, *refs):
    x_refs, refs = refs[:chunks], refs[chunks:]
    if last:
        prev_ref, q_ref, k_ref, v_ref, keep_ref, send_ref, acc_ref = refs
    else:
        q_ref, k_ref, v_ref, grad_ref, acc_ref = refs
    step = pl.program_id(0)
    tile = q_ref.shape[0]
    cols = heads * dim
    units = ft_ref.shape[2]

    @pl.when(step == 0)
    def _():
        acc_ref[...] = jnp.zeros_like(acc_ref)

    x = x_refs[0][...]
    for c in range(1, chunks):
        x = jnp.where(step >= c * steps, x_refs[c][...], x)
    packed = mm(wt_ref[...], x, 1, 1).astype(BF16)
    place = ((base + step // steps) ^ ids_ref[1]) * tokens + (step % steps) * tile
    mask = -(mask_ref[:, pl.ds(pl.multiple_of(place, tile), tile)].astype(F32))
    queries, keys, values, targets = [], [], [], []
    for h in range(heads):
        rows = slice(h * dim, (h + 1) * dim)
        queries.append(unit(packed[:cols][rows].astype(F32), 0).astype(BF16))
        keys.append(unit(packed[cols : 2 * cols][rows].astype(F32), 0).astype(BF16))
        value = packed[2 * cols :][rows]
        values.append(value)
        targets.append((value.astype(F32) * mask).astype(BF16))
    q_ref[...] = jnp.concatenate(queries, axis=0).T
    k_ref[...] = jnp.concatenate(keys, axis=0)
    turned = jnp.concatenate(values, axis=0).T
    ones = jnp.ones((tile, dim), BF16)
    for h in range(heads):
        v_ref[h] = jnp.concatenate([turned[:, h * dim : (h + 1) * dim], ones], axis=1)
    width = min(256, units)
    for h in range(heads):
        for c in range(0, units, width):
            part = slice(c, c + width)
            first = mm(ft_ref[h, 0, part], keys[h], 1, 0)
            third = mm(ft_ref[h, 1, part], keys[h], 1, 0)
            back = mm(ft_ref[h, 2, part], targets[h], 1, 0)
            sigma = sigmoid(first)
            silu = first * sigma
            hidden = (silu * third).astype(BF16)
            d_third = (back * silu).astype(BF16)
            d_first = (back * third * (sigma + silu * (1.0 - sigma))).astype(BF16)
            acc_ref[h, 0, part] += mm(d_first, keys[h], 1, 1)
            acc_ref[h, 1, part] += mm(d_third, keys[h], 1, 1)
            acc_ref[h, 2, part] += mm(hidden, targets[h], 1, 1)

    @pl.when(step == pl.num_programs(0) - 1)
    def _():
        for h in range(heads):
            if not last:
                for j in range(3):
                    grad_ref[h, j] = acc_ref[h, j].T
                continue
            total = [(acc_ref[h, j].T + prev_ref[h, j]).astype(BF16) for j in range(3)]
            pair = [total[:2], [total[2], jnp.zeros_like(total[2])]]
            for low in range(2):

                @pl.when((ids_ref[0] & 1) == low)
                def _():
                    for i in range(2):
                        keep_ref[h, i] = pair[low][i]
                        send_ref[h, i] = pair[1 - low][i]


def front(ids, xs, base, wt, ft, mask, prev=None):
    tokens, depth = xs[0].shape
    heads, _, units, dim = ft.shape
    cols = heads * dim
    tile = min(512, tokens)
    steps = tokens // tile
    chunks = len(xs)
    total = chunks * tokens
    last = prev is not None

    def pick(c):
        return lambda i: (jnp.clip(i - c * steps, 0, steps - 1), 0)

    in_specs = [SMEM, whole(mask.shape), whole(wt.shape), whole(ft.shape)]
    in_specs += [pl.BlockSpec((tile, depth), pick(c)) for c in range(chunks)]
    out_specs = [
        pl.BlockSpec((tile, cols), lambda i: (i, 0)),
        pl.BlockSpec((cols, tile), lambda i: (0, i)),
        pl.BlockSpec((heads, tile, 2 * dim), lambda i: (0, i, 0)),
    ]
    out_shape = [
        jax.ShapeDtypeStruct((total, cols), BF16),
        jax.ShapeDtypeStruct((cols, total), BF16),
        jax.ShapeDtypeStruct((heads, total, 2 * dim), BF16),
    ]
    args = [ids, mask, wt, ft, *xs]
    if last:
        in_specs.append(whole(prev.shape))
        args.append(prev)
        out_specs += [whole((heads, 2, dim, units))] * 2
        out_shape += [jax.ShapeDtypeStruct((heads, 2, dim, units), BF16)] * 2
    else:
        out_specs.append(whole((heads, 3, dim, units)))
        out_shape.append(jax.ShapeDtypeStruct((heads, 3, dim, units), F32))
    return pl.pallas_call(
        functools.partial(front_kernel, heads, dim, chunks, steps, base, tokens, last),
        grid=(chunks * steps,),
        in_specs=in_specs,
        out_specs=out_specs,
        out_shape=out_shape,
        scratch_shapes=[pltpu.VMEM((heads, 3, units, dim), F32)],
        cost_estimate=cost(4 * total * cols * 2 * (3 * depth + 6 * units), 6 * 2**20),
        name="front",
    )(*args)


def attend_kernel(heads, dim, halves, q_ref, *refs):
    k_refs, v_refs, o_ref = refs[:halves], refs[halves : 2 * halves], refs[2 * halves]
    outs = []
    for h in range(heads):
        rows = slice(h * dim, (h + 1) * dim)
        query = q_ref[:, rows]
        total = None
        for k_ref, v_ref in zip(k_refs, v_refs):
            span = k_ref.shape[1]
            width = min(512, span)
            for c in range(0, span, width):
                scores = mm(query, k_ref[rows, c : c + width], 1, 0)
                probs = jnp.exp2(scores * (score_scale * log2_e)).astype(BF16)
                part = mm(probs, v_ref[h, c : c + width], 1, 0)
                total = part if total is None else total + part
        outs.append(total[:, :dim] / total[:, dim:])
    o_ref[...] = jnp.concatenate(outs, axis=1).astype(BF16)


def attend(q, ks, vs):
    total, cols = q.shape
    heads, _, twice = vs[0].shape
    tile = min(512, total)
    keys = sum(k.shape[1] for k in ks)
    return pl.pallas_call(
        functools.partial(attend_kernel, heads, twice // 2, len(ks)),
        grid=(total // tile,),
        in_specs=[pl.BlockSpec((tile, cols), lambda i: (i, 0))] + [whole(a.shape) for a in (*ks, *vs)],
        out_specs=pl.BlockSpec((tile, cols), lambda i: (i, 0)),
        out_shape=jax.ShapeDtypeStruct((total, cols), BF16),
        cost_estimate=cost(4 * 4 * total * keys * cols, 4 * 2**20),
        name="attend",
    )(q, *ks, *vs)


def newton_kernel(count, ids_ref, ft_ref, *refs):
    parts, o_ref = refs[:count], refs[count]
    heads = ft_ref.shape[0]
    exact = lax.Precision.HIGHEST
    head = lax.rem(ids_ref[0] >> 1, heads)
    for i in range(2):
        total = parts[0][i].astype(F32)
        for part in parts[1:]:
            total += part[i].astype(F32)
        current = total * lax.rsqrt(jnp.sum(total * total, keepdims=True) + 1e-06)
        for _ in range(NS_STEPS):
            gram = mm(current, current, 1, 1, exact)
            squared = mm(gram, gram, 1, 0, exact)
            polynomial = newton_coeffs[1] * gram + newton_coeffs[2] * squared
            current = newton_coeffs[0] * current + mm(polynomial, current, 1, 0, exact)
        which = jnp.minimum(2 * (ids_ref[0] & 1) + i, 2)
        initial = ft_ref[head, which].astype(F32).T
        o_ref[i] = (initial - learn_rate * current).astype(BF16)


def newton(ids, ft, parts):
    return pl.pallas_call(
        functools.partial(newton_kernel, len(parts)),
        grid=(1,),
        in_specs=[SMEM, whole(ft.shape)] + [whole(p.shape) for p in parts],
        out_specs=whole(parts[0].shape),
        out_shape=jax.ShapeDtypeStruct(parts[0].shape, BF16),
        cost_estimate=cost(2**30, 4 * 2**20),
        name="newton",
    )(ids, ft, *parts)


def apply_kernel(heads, dim, count, ids_ref, q_ref, a_ref, *refs):
    mine, other, (o_ref, fast_ref) = refs[:count], refs[count : 2 * count], refs[2 * count :]
    units = fast_ref.shape[3]

    @pl.when(pl.program_id(0) == 0)
    def _():
        low = ids_ref[0] & 1
        for k in range(count):
            head = (ids_ref[0] >> 1) ^ k

            @pl.when(head < heads)
            def _():
                for i in range(2):
                    fast_ref[head, 2 * low + i] = mine[k][i]
                    fast_ref[head, 2 - 2 * low + i] = other[k][i]

    outs = []
    for h in range(heads):
        query = q_ref[:, h * dim : (h + 1) * dim]
        first = mm(query, fast_ref[h, 0], 1, 0)
        third = mm(query, fast_ref[h, 1], 1, 0)
        hidden = (first * sigmoid(first) * third).astype(BF16)
        outs.append(unit(mm(hidden, fast_ref[h, 2], 1, 1), 1))
    o_ref[...] = (jnp.concatenate(outs, axis=1) + a_ref[...].astype(F32)).astype(BF16)


def apply_fast(ids, q, attended, mine, other, heads):
    total, cols = q.shape
    dim = cols // heads
    units = mine[0].shape[2]
    tile = min(512, total)
    return pl.pallas_call(
        functools.partial(apply_kernel, heads, dim, len(mine)),
        grid=(total // tile,),
        in_specs=[SMEM]
        + [pl.BlockSpec((tile, cols), lambda i: (i, 0))] * 2
        + [whole(a.shape) for a in (*mine, *other)],
        out_specs=pl.BlockSpec((tile, cols), lambda i: (i, 0)),
        out_shape=jax.ShapeDtypeStruct((total, cols), BF16),
        scratch_shapes=[pltpu.VMEM((heads, 4, dim, units), BF16)],
        cost_estimate=cost(4 * 2 * total * cols * units * 3, 4 * 2**20),
        name="apply",
    )(ids, q, attended, *mine, *other)


def order_kernel(count, ids_ref, *refs):
    own, pair, o_ref = refs[:count], refs[count], refs[count + 1]
    rows = own[0].shape[0]
    low = ids_ref[1] & 1
    for k in range(count):
        slab = (ids_ref[0] ^ k) * 2
        o_ref[pl.ds(pl.multiple_of((slab + low) * rows, rows), rows)] = own[k][...]
        o_ref[pl.ds(pl.multiple_of((slab + 1 - low) * rows, rows), rows)] = pair[k * rows : (k + 1) * rows]


def order_rows(ids, own, pair):
    rows, width = own[0].shape
    shape = (2 * len(own) * rows, width)
    return pl.pallas_call(
        functools.partial(order_kernel, len(own)),
        grid=(1,),
        in_specs=[SMEM] + [whole(a.shape) for a in (*own, pair)],
        out_specs=whole(shape),
        out_shape=jax.ShapeDtypeStruct(shape, BF16),
        cost_estimate=cost(0, 4 * 2**20),
        name="order",
    )(ids, *own, pair)


def project_kernel(count, more, ids_ref, s_ref, w_ref, *refs):
    parts, outs = refs[:count], refs[count:]
    cols = parts[0].shape[1]
    total = s_ref[...].astype(F32)
    projected = None
    for k in range(count):
        place = pl.multiple_of((ids_ref[1] ^ k) * cols, cols)
        part = mm(parts[k][...], w_ref[pl.ds(place, cols)], 1, 0)
        projected = part if projected is None else projected + part
    stream = (total + projected).astype(BF16)
    outs[0][...] = stream
    if more:
        outs[1][...] = unit(stream.astype(F32), 1).astype(BF16)


def project(ids, stream, weight, parts, starts, more):
    tokens, depth = stream.shape
    tile = min(256, tokens)
    cols = parts[0].shape[1]
    count = 2 if more else 1

    def pick(start):
        return lambda i: (start // tile + i, 0)

    return pl.pallas_call(
        functools.partial(project_kernel, len(parts), more),
        grid=(tokens // tile,),
        in_specs=[SMEM, pl.BlockSpec((tile, depth), lambda i: (i, 0)), whole(weight.shape)]
        + [pl.BlockSpec((tile, cols), pick(s)) for s in starts],
        out_specs=[pl.BlockSpec((tile, depth), lambda i: (i, 0))] * count,
        out_shape=[jax.ShapeDtypeStruct((tokens, depth), BF16)] * count,
        cost_estimate=cost(2 * tokens * depth * depth, 6 * 2**20),
        name="project",
    )(ids, stream, weight, *parts)


def solution(mesh):
    views, parts = mesh.shape["view"], mesh.shape["head"]

    def swap(x, axis, k, keep=None):
        pairs = [(i, i ^ k) for i in range(mesh.shape[axis])]
        if keep is not None:
            pairs = [p for p in pairs if keep(*p)]
        return lax.ppermute(x, axis, pairs)

    def gather_view(block):
        slabs = {0: block}
        slabs[1] = swap(block, "view", 1)
        for k in range(2, views, 2):
            slabs[k] = swap(block, "view", k)
            slabs[k + 1] = swap(slabs[k], "view", 1)
        return [slabs[k] for k in range(views)]

    def shards(features, attend_weight, output_weight, fast_init, update_mask):
        blocks, _, d_slab, cols = attend_weight.shape
        heads, dim, f_slab = fast_init.shape[1], fast_init.shape[3], fast_init.shape[4]
        tokens = features.shape[0]
        ids = jnp.stack([lax.axis_index("view"), lax.axis_index("head")]).astype(jnp.int32)
        low = ids[1] & 1
        fast_rows = fast_init.transpose(0, 2, 4, 1, 3).reshape(blocks, 3 * f_slab, cols)
        packed = jnp.concatenate([attend_weight.reshape(blocks, 3 * d_slab, cols), fast_rows], axis=1)
        out_rows = output_weight.shape[1] // 2
        own_rows = lax.dynamic_slice_in_dim(output_weight, low * out_rows, out_rows, 1)

        stream = features
        normed = unit(features.astype(F32), 1).astype(BF16)
        for layer in range(blocks):
            xs = [normed]
            for k in range(1, parts):
                high = 1 << (k.bit_length() - 1)
                xs.append(swap(xs[k ^ high], "head", high) if high == k else swap(xs[high], "head", k ^ high))
            slabs = gather_view(packed[layer])
            wt, ft = prepare(ids, slabs, d_slab, f_slab, heads, dim)
            half = parts // 2
            qa, ka, va, prev = front(ids, xs[:half], 0, wt, ft, update_mask)
            qb, kb, vb, keep, send = front(ids, xs[half:], half, wt, ft, update_mask, prev)
            got = swap(send, "view", 1)
            summed = (keep.astype(F32) + got.astype(F32)).astype(BF16)
            place = ids[0] >> 1
            pieces = []
            for k in range(views // 2):
                part = lax.dynamic_index_in_dim(summed, lax.rem(place ^ k, heads), 0, keepdims=False)
                if k:
                    part = swap(part, "view", 2 * k, lambda i, o: (o >> 1) < heads)
                pieces.append(part)
            attended_b = attend(qb, [ka, kb], [va, vb])
            attended_a = attend(qa, [ka, kb], [va, vb])
            fresh = newton(ids, ft, pieces)
            mine = [fresh] + [
                swap(fresh, "view", 2 * k, lambda i, o: (i >> 1) < heads) for k in range(1, views // 2)
            ]
            other = [swap(m, "view", 1) for m in mine]
            mixed_b = apply_fast(ids, qb, attended_b, mine, other, heads)
            mixed_a = apply_fast(ids, qa, attended_a, mine, other, heads)
            received, starts = [mixed_a], [0]
            for k in range(1, parts):
                source, at = (mixed_a, k) if k < half else (mixed_b, k - half)
                received.append(swap(source[at * tokens : (at + 1) * tokens], "head", k))
                starts.append(0)
            own = gather_view(own_rows[layer])
            pair = swap(jnp.concatenate(own, axis=0), "head", 1)
            weight = order_rows(ids, own, pair)
            more = layer + 1 < blocks
            result = project(ids, stream, weight, received, starts, more)
            stream = result[0]
            normed = result[-1]
        return stream

    return jax.shard_map(
        shards,
        mesh=mesh,
        in_specs=(
            P(("view", "head"), None),
            P(None, None, "view", "head"),
            P(None, "view", None),
            P(None, "head", None, None, "view"),
            P("view", None),
        ),
        out_specs=P(("view", "head"), None),
        check_vma=False,
    )
```

```python
import functools
import math

import jax
import jax.numpy as jnp
from jax import lax
from jax.experimental import pallas as pl
from jax.experimental.pallas import tpu as pltpu
from jax.sharding import PartitionSpec as P


NS_STEPS = 5

newton_coeffs = (3.4445, -4.775, 2.0315)
learn_rate = 1.0
score_scale = 0.25
log2_e = math.log2(math.e)

F32, BF16 = jnp.float32, jnp.bfloat16
SMEM = pl.BlockSpec(memory_space=pltpu.SMEM)


def mm(a, b, ca, cb, precision=None):
    return lax.dot_general(
        a, b, (((ca,), (cb,)), ((), ())), preferred_element_type=F32, precision=precision
    )


def whole(shape):
    return pl.BlockSpec(tuple(shape), lambda i: (0,) * len(shape))


def cost(flops, nbytes, trans=0):
    return pl.CostEstimate(flops=int(flops), bytes_accessed=int(nbytes), transcendentals=int(trans))


def sigmoid(x):
    return 0.5 * jnp.tanh(0.5 * x) + 0.5


def unit(part, axis):
    return part * lax.rsqrt(jnp.mean(part * part, axis=axis, keepdims=True) + 1e-05)


def prepare_kernel(count, d_slab, f_slab, heads, dim, ids_ref, *refs):
    slabs, (wt_ref, ft_ref), (w_all, f_all) = refs[:count], refs[count : count + 2], refs[count + 2 :]
    cols = heads * dim
    for k in range(count):
        source = ids_ref[0] ^ k
        for j in range(3):
            w_all[j, pl.ds(pl.multiple_of(source * d_slab, d_slab), d_slab)] = slabs[k][
                j * d_slab : (j + 1) * d_slab
            ]
            f_all[j, pl.ds(pl.multiple_of(source * f_slab, f_slab), f_slab)] = slabs[k][
                3 * d_slab + j * f_slab : 3 * d_slab + (j + 1) * f_slab
            ]
    for j in range(3):
        wt_ref[j * cols : (j + 1) * cols] = w_all[j].T
        for h in range(heads):
            ft_ref[h, j] = f_all[j, :, h * dim : (h + 1) * dim]


def prepare(ids, slabs, d_slab, f_slab, heads, dim):
    count = len(slabs)
    cols = heads * dim
    depth, units = count * d_slab, count * f_slab
    return pl.pallas_call(
        functools.partial(prepare_kernel, count, d_slab, f_slab, heads, dim),
        grid=(1,),
        in_specs=[SMEM] + [whole(s.shape) for s in slabs],
        out_specs=[whole((3 * cols, depth)), whole((heads, 3, units, dim))],
        out_shape=[
            jax.ShapeDtypeStruct((3 * cols, depth), BF16),
            jax.ShapeDtypeStruct((heads, 3, units, dim), BF16),
        ],
        scratch_shapes=[pltpu.VMEM((3, depth, cols), BF16), pltpu.VMEM((3, units, cols), BF16)],
        cost_estimate=cost(0, 8 * 2**20),
        name="prepare",
    )(ids, *slabs)


def front_kernel(heads, dim, chunks, steps, base, tokens, last, ids_ref, mask_ref, wt_ref, ft_ref, *refs):
    x_refs, refs = refs[:chunks], refs[chunks:]
    if last:
        prev_ref, q_ref, k_ref, v_ref, grad_ref, acc_ref = refs
    else:
        q_ref, k_ref, v_ref, grad_ref, acc_ref = refs
    step = pl.program_id(0)
    tile = q_ref.shape[0]
    cols = heads * dim
    units = ft_ref.shape[2]

    @pl.when(step == 0)
    def _():
        acc_ref[...] = jnp.zeros_like(acc_ref)

    x = x_refs[0][...]
    for c in range(1, chunks):
        x = jnp.where(step >= c * steps, x_refs[c][...], x)
    packed = mm(wt_ref[...], x, 1, 1).astype(BF16)
    place = ((base + step // steps) ^ ids_ref[1]) * tokens + (step % steps) * tile
    mask = -(mask_ref[:, pl.ds(pl.multiple_of(place, tile), tile)].astype(F32))
    queries, keys, values, targets = [], [], [], []
    for h in range(heads):
        rows = slice(h * dim, (h + 1) * dim)
        queries.append(unit(packed[:cols][rows].astype(F32), 0).astype(BF16))
        keys.append(unit(packed[cols : 2 * cols][rows].astype(F32), 0).astype(BF16))
        value = packed[2 * cols :][rows]
        values.append(value)
        targets.append((value.astype(F32) * mask).astype(BF16))
    q_ref[...] = jnp.concatenate(queries, axis=0).T
    k_ref[...] = jnp.concatenate(keys, axis=0)
    turned = jnp.concatenate(values, axis=0).T
    ones = jnp.ones((tile, dim), BF16)
    for h in range(heads):
        v_ref[h] = jnp.concatenate([turned[:, h * dim : (h + 1) * dim], ones], axis=1)
    width = min(256, units)
    for h in range(heads):
        for c in range(0, units, width):
            part = slice(c, c + width)
            first = mm(ft_ref[h, 0, part], keys[h], 1, 0)
            third = mm(ft_ref[h, 1, part], keys[h], 1, 0)
            back = mm(ft_ref[h, 2, part], targets[h], 1, 0)
            sigma = sigmoid(first)
            silu = first * sigma
            hidden = (silu * third).astype(BF16)
            d_third = (back * silu).astype(BF16)
            d_first = (back * third * (sigma + silu * (1.0 - sigma))).astype(BF16)
            acc_ref[h, 0, part] += mm(d_first, keys[h], 1, 1)
            acc_ref[h, 1, part] += mm(d_third, keys[h], 1, 1)
            acc_ref[h, 2, part] += mm(hidden, targets[h], 1, 1)

    @pl.when(step == pl.num_programs(0) - 1)
    def _():
        for h in range(heads):
            for j in range(3):
                rows = slice(j * dim, (j + 1) * dim)
                total = acc_ref[h, j].T
                if last:
                    slot = h ^ lax.rem(ids_ref[0] >> 1, heads)
                    grad_ref[slot, rows] = (total + prev_ref[h, rows]).astype(BF16)
                else:
                    grad_ref[h, rows] = total


def front(ids, xs, base, wt, ft, mask, prev=None):
    tokens, depth = xs[0].shape
    heads, _, units, dim = ft.shape
    cols = heads * dim
    tile = min(512, tokens)
    steps = tokens // tile
    chunks = len(xs)
    total = chunks * tokens
    last = prev is not None

    def pick(c):
        return lambda i: (jnp.clip(i - c * steps, 0, steps - 1), 0)

    in_specs = [SMEM, whole(mask.shape), whole(wt.shape), whole(ft.shape)]
    in_specs += [pl.BlockSpec((tile, depth), pick(c)) for c in range(chunks)]
    out_specs = [
        pl.BlockSpec((tile, cols), lambda i: (i, 0)),
        pl.BlockSpec((cols, tile), lambda i: (0, i)),
        pl.BlockSpec((heads, tile, 2 * dim), lambda i: (0, i, 0)),
    ]
    out_shape = [
        jax.ShapeDtypeStruct((total, cols), BF16),
        jax.ShapeDtypeStruct((cols, total), BF16),
        jax.ShapeDtypeStruct((heads, total, 2 * dim), BF16),
    ]
    args = [ids, mask, wt, ft, *xs]
    if last:
        in_specs.append(whole(prev.shape))
        args.append(prev)
    out_specs.append(whole((heads, 3 * dim, units)))
    out_shape.append(jax.ShapeDtypeStruct((heads, 3 * dim, units), BF16 if last else F32))
    return pl.pallas_call(
        functools.partial(front_kernel, heads, dim, chunks, steps, base, tokens, last),
        grid=(chunks * steps,),
        in_specs=in_specs,
        out_specs=out_specs,
        out_shape=out_shape,
        scratch_shapes=[pltpu.VMEM((heads, 3, units, dim), F32)],
        cost_estimate=cost(4 * total * cols * 2 * (3 * depth + 6 * units), 6 * 2**20),
        name="front",
    )(*args)


def attend_kernel(heads, dim, halves, q_ref, *refs):
    k_refs, v_refs, o_ref = refs[:halves], refs[halves : 2 * halves], refs[2 * halves]
    outs = []
    for h in range(heads):
        rows = slice(h * dim, (h + 1) * dim)
        query = q_ref[:, rows]
        total = None
        for k_ref, v_ref in zip(k_refs, v_refs):
            span = k_ref.shape[1]
            width = min(512, span)
            for c in range(0, span, width):
                scores = mm(query, k_ref[rows, c : c + width], 1, 0)
                probs = jnp.exp2(scores * (score_scale * log2_e)).astype(BF16)
                part = mm(probs, v_ref[h, c : c + width], 1, 0)
                total = part if total is None else total + part
        outs.append(total[:, :dim] / total[:, dim:])
    o_ref[...] = jnp.concatenate(outs, axis=1).astype(BF16)


def attend(q, ks, vs, start, total):
    cols = q.shape[1]
    heads, _, twice = vs[0].shape
    tile = min(512, total)
    keys = sum(k.shape[1] for k in ks)
    return pl.pallas_call(
        functools.partial(attend_kernel, heads, twice // 2, len(ks)),
        grid=(total // tile,),
        in_specs=[pl.BlockSpec((tile, cols), lambda i: (start // tile + i, 0))]
        + [whole(a.shape) for a in (*ks, *vs)],
        out_specs=pl.BlockSpec((tile, cols), lambda i: (i, 0)),
        out_shape=jax.ShapeDtypeStruct((total, cols), BF16),
        cost_estimate=cost(4 * 4 * total * keys * cols, 4 * 2**20),
        name="attend",
    )(q, *ks, *vs)


def split(x):
    high = x.astype(BF16)
    return high, (x - high.astype(F32)).astype(BF16)


def mm_split(a, b, ca, cb):
    return mm(a[0], b[0], ca, cb) + (mm(a[0], b[1], ca, cb) + mm(a[1], b[0], ca, cb))


def newton_kernel(ids_ref, ft_ref, own_ref, got_ref, o_ref):
    heads, _, _, dim = ft_ref.shape
    head = lax.rem(ids_ref[0] >> 1, heads)
    summed = own_ref[...].astype(F32) + got_ref[...].astype(F32)
    scaled = []
    for j in range(3):
        total = summed[j * dim : (j + 1) * dim]
        scaled.append(total * lax.rsqrt(jnp.sum(total * total, keepdims=True) + 1e-06))
    current = jnp.concatenate(scaled, axis=0)
    side = lax.broadcasted_iota(jnp.int32, (3 * dim, 3 * dim), 0) // dim
    same = side == lax.broadcasted_iota(jnp.int32, (3 * dim, 3 * dim), 1) // dim
    for _ in range(NS_STEPS):
        halves = split(current)
        gram = jnp.where(same, mm_split(halves, halves, 1, 1), 0.0)
        parts = split(gram)
        polynomial = newton_coeffs[1] * gram + newton_coeffs[2] * mm_split(parts, parts, 1, 0)
        current = newton_coeffs[0] * current + mm_split(split(polynomial), halves, 1, 0)
    for j in range(3):
        rows = slice(j * dim, (j + 1) * dim)
        initial = ft_ref[head, j].astype(F32).T
        o_ref[rows] = (initial - learn_rate * current[rows]).astype(BF16)


def newton(ids, ft, own, got):
    return pl.pallas_call(
        newton_kernel,
        grid=(1,),
        in_specs=[SMEM, whole(ft.shape), whole(own.shape), whole(got.shape)],
        out_specs=whole(own.shape),
        out_shape=jax.ShapeDtypeStruct(own.shape, BF16),
        cost_estimate=cost(2**30, 4 * 2**20),
        name="newton",
    )(ids, ft, own, got)


def apply_kernel(heads, dim, count, spans, ids_ref, q_ref, *refs):
    a_refs, refs = refs[: len(spans)], refs[len(spans) :]
    units_refs, (o_ref, fast_ref) = refs[:count], refs[count:]

    @pl.when(pl.program_id(0) == 0)
    def _():
        for k in range(count):
            head = (ids_ref[0] >> 1) ^ k

            @pl.when(head < heads)
            def _():
                fast_ref[head] = units_refs[k][...]

    attended = a_refs[0][...]
    for at, a_ref in zip(spans[1:], a_refs[1:]):
        attended = jnp.where(pl.program_id(0) >= at, a_ref[...], attended)
    outs = []
    for h in range(heads):
        query = q_ref[:, h * dim : (h + 1) * dim]
        first = mm(query, fast_ref[h, :dim], 1, 0)
        third = mm(query, fast_ref[h, dim : 2 * dim], 1, 0)
        hidden = (first * sigmoid(first) * third).astype(BF16)
        outs.append(unit(mm(hidden, fast_ref[h, 2 * dim :], 1, 1), 1))
    o_ref[...] = (jnp.concatenate(outs, axis=1) + attended.astype(F32)).astype(BF16)


def apply_fast(ids, q, attended, fast, heads):
    total, cols = q.shape
    dim = cols // heads
    units = fast[0].shape[1]
    tile = min(512, *(a.shape[0] for a in attended))
    spans, steps = [], 0
    in_specs = [SMEM, pl.BlockSpec((tile, cols), lambda i: (i, 0))]
    for a in attended:
        here = a.shape[0] // tile
        in_specs.append(pl.BlockSpec((tile, cols), lambda i, s=steps, n=here: (jnp.clip(i - s, 0, n - 1), 0)))
        spans.append(steps)
        steps += here
    return pl.pallas_call(
        functools.partial(apply_kernel, heads, dim, len(fast), tuple(spans)),
        grid=(total // tile,),
        in_specs=in_specs + [whole(a.shape) for a in fast],
        out_specs=pl.BlockSpec((tile, cols), lambda i: (i, 0)),
        out_shape=jax.ShapeDtypeStruct((total, cols), BF16),
        scratch_shapes=[pltpu.VMEM((heads, 3 * dim, units), BF16)],
        cost_estimate=cost(4 * 2 * total * cols * units * 3, 4 * 2**20),
        name="apply",
    )(ids, q, *attended, *fast)


def order_kernel(ids_ref, *refs):
    slabs, o_ref = refs[:-1], refs[-1]
    rows = slabs[0].shape[0]
    for k, slab in enumerate(slabs):
        o_ref[pl.ds(pl.multiple_of((ids_ref[0] ^ k) * rows, rows), rows)] = slab[...]


def order_rows(ids, slabs):
    rows, width = slabs[0].shape
    shape = (len(slabs) * rows, width)
    return pl.pallas_call(
        order_kernel,
        grid=(1,),
        in_specs=[SMEM] + [whole(a.shape) for a in slabs],
        out_specs=whole(shape),
        out_shape=jax.ShapeDtypeStruct(shape, BF16),
        cost_estimate=cost(0, 2 * 2**20),
        name="order",
    )(ids, *slabs)


def project_kernel(count, more, ids_ref, s_ref, own_ref, pair_ref, *refs):
    parts, outs = refs[:count], refs[count:]
    cols = parts[0].shape[1]
    half = own_ref.shape[1]
    low = ids_ref[1] & 1
    for which, w_ref in ((low, own_ref), (1 - low, pair_ref)):
        projected = None
        for k in range(count):
            place = pl.multiple_of((ids_ref[1] ^ k) * cols, cols)
            part = mm(parts[k][...], w_ref[pl.ds(place, cols)], 1, 0)
            projected = part if projected is None else projected + part
        here = pl.ds(pl.multiple_of(which * half, half), half)
        outs[0][:, here] = (s_ref[:, here].astype(F32) + projected).astype(BF16)
    if more:
        outs[1][...] = unit(outs[0][...].astype(F32), 1).astype(BF16)


def project(ids, stream, own, pair, parts, more):
    tokens, depth = stream.shape
    tile = min(256, tokens)
    cols = parts[0].shape[1]
    count = 2 if more else 1
    return pl.pallas_call(
        functools.partial(project_kernel, len(parts), more),
        grid=(tokens // tile,),
        in_specs=[SMEM, pl.BlockSpec((tile, depth), lambda i: (i, 0)), whole(own.shape), whole(pair.shape)]
        + [pl.BlockSpec((tile, cols), lambda i: (i, 0))] * len(parts),
        out_specs=[pl.BlockSpec((tile, depth), lambda i: (i, 0))] * count,
        out_shape=[jax.ShapeDtypeStruct((tokens, depth), BF16)] * count,
        cost_estimate=cost(2 * tokens * depth * depth, 6 * 2**20),
        name="project",
    )(ids, stream, own, pair, *parts)


def solution(mesh):
    views, parts = mesh.shape["view"], mesh.shape["head"]

    def swap(x, axis, k, keep=None):
        pairs = [(i, i ^ k) for i in range(mesh.shape[axis])]
        if keep is not None:
            pairs = [p for p in pairs if keep(*p)]
        return lax.ppermute(x, axis, pairs)

    def gather_view(block):
        slabs = {0: block}
        for k in range(2, views, 2):
            slabs[k] = swap(block, "view", k)
        for k in range(0, views, 2):
            slabs[k + 1] = swap(slabs[k], "view", 1)
        return [slabs[k] for k in range(views)]

    def shards(features, attend_weight, output_weight, fast_init, update_mask):
        blocks, _, d_slab, cols = attend_weight.shape
        heads, dim, f_slab = fast_init.shape[1], fast_init.shape[3], fast_init.shape[4]
        tokens = features.shape[0]
        half = parts // 2
        ids = jnp.stack([lax.axis_index("view"), lax.axis_index("head")]).astype(jnp.int32)
        fast_rows = fast_init.transpose(0, 2, 4, 1, 3).reshape(blocks, 3 * f_slab, cols)
        packed = jnp.concatenate([attend_weight.reshape(blocks, 3 * d_slab, cols), fast_rows], axis=1)
        wide = output_weight.shape[2] // 2
        own_columns = lax.dynamic_slice_in_dim(output_weight, (ids[1] & 1) * wide, wide, 2)

        stream = features
        normed = unit(features.astype(F32), 1).astype(BF16)
        for layer in range(blocks):
            slabs = gather_view(packed[layer])
            xs = [normed]
            for k in range(1, parts):
                high = 1 << (k.bit_length() - 1)
                from_k, hop = (0, k) if high == k else (high, k ^ high)
                xs.append(swap(xs[from_k], "head", hop))
            wt, ft = prepare(ids, slabs, d_slab, f_slab, heads, dim)
            qa, ka, va, prev = front(ids, xs[:half], 0, wt, ft, update_mask)
            qb, kb, vb, grads = front(ids, xs[half:], half, wt, ft, update_mask, prev)
            near = grads[0].astype(F32)
            for k in range(1, views // 2):
                part = swap(grads[k % heads], "view", 2 * k, lambda i, o: (o >> 1) < heads)
                near = near + part.astype(F32)
            near = near.astype(BF16)
            got = swap(near, "view", 1)
            ks, vs = [ka, kb], [va, vb]
            count = qb.shape[0]
            attended_b = [attend(qb, ks, vs, 0, count)]
            attended_a = []
            for i in range(2):
                attended_a.append(attend(qa, ks, vs, i * count // 2, count // 2))
            fresh = newton(ids, ft, near, got)
            fast = [fresh] + [
                swap(fresh, "view", 2 * k, lambda i, o: (i >> 1) < heads)
                for k in range(1, views // 2)
            ]
            mixed_b = apply_fast(ids, qb, attended_b, fast, heads)
            mixed_a = apply_fast(ids, qa, attended_a, fast, heads)
            received = [mixed_a]
            for k in range(1, parts):
                source, row = (mixed_a, k) if k < half else (mixed_b, k - half)
                received.append(swap(source[row * tokens : (row + 1) * tokens], "head", k))
            own = order_rows(ids, gather_view(own_columns[layer]))
            pair = swap(own, "head", 1)
            more = layer + 1 < blocks
            result = project(ids, stream, own, pair, received, more)
            stream = result[0]
            normed = result[-1]
        return stream


    return jax.shard_map(
        shards,
        mesh=mesh,
        in_specs=(
            P(("view", "head"), None),
            P(None, None, "view", "head"),
            P(None, "view", None),
            P(None, "head", None, None, "view"),
            P("view", None),
        ),
        out_specs=P(("view", "head"), None),
        check_vma=False,
    )
```

```python
import functools
import math

import jax
import jax.numpy as jnp
from jax import lax
from jax.experimental import pallas as pl
from jax.experimental.pallas import tpu as pltpu
from jax.sharding import PartitionSpec as P


NS_STEPS = 5

newton_coeffs = (3.4445, -4.775, 2.0315)
learn_rate = 1.0
score_scale = 0.25
log2_e = math.log2(math.e)

F32, BF16 = jnp.float32, jnp.bfloat16
SMEM = pl.BlockSpec(memory_space=pltpu.SMEM)

FRONT_TILE, FRONT_WIDTH, FRONT_UNROLL, FRONT_TYPE = 256, 512, 4, F32
APPLY_TILE, APPLY_TYPE = 512, F32
VMEM_MIB = 32
ATTEND_TILE, ATTEND_WIDTH, ATTEND_UNROLL = 256, 1024, False


def mm(a, b, ca, cb, precision=None):
    return lax.dot_general(
        a, b, (((ca,), (cb,)), ((), ())), preferred_element_type=F32, precision=precision
    )


def whole(shape):
    return pl.BlockSpec(tuple(shape), lambda i: (0,) * len(shape))


def cost(flops, nbytes, trans=0):
    return pl.CostEstimate(flops=int(flops), bytes_accessed=int(nbytes), transcendentals=int(trans))


def sigmoid(x):
    return 0.5 * jnp.tanh(0.5 * x) + 0.5


def unit(part, axis):
    return part * lax.rsqrt(jnp.mean(part * part, axis=axis, keepdims=True) + 1e-05)


LIMIT = pltpu.CompilerParams(vmem_limit_bytes=VMEM_MIB * 2**20)
ANY = pl.BlockSpec(memory_space=pl.ANY)


def pack_kernel(wide, ids_ref, w_ref, f_ref, o_ref, *outs):
    blocks, _, d_slab, cols = w_ref.shape
    heads = f_ref.shape[1]
    f_slab = f_ref.shape[4]
    rows = o_ref.shape[1]
    for b in range(blocks):
        at = 3 * d_slab
        for j in range(3):
            outs[b][j * d_slab : (j + 1) * d_slab] = w_ref[b, j]
            parts = [f_ref[b, h, j].astype(F32).T for h in range(heads)]
            outs[b][at : at + f_slab] = jnp.concatenate(parts, axis=1).astype(BF16)
            at += f_slab
        for i in range(blocks if b == 1 else 0):
            for c in range(0, wide, cols):
                place = pl.multiple_of((ids_ref[1] & 1) * wide + c, cols)
                outs[b][at : at + rows] = o_ref[i, :, pl.ds(place, cols)]
                at += rows


def pack(ids, weight, fast, output):
    blocks, _, d_slab, cols = weight.shape
    f_slab = fast.shape[4]
    rows, wide = output.shape[1], output.shape[2] // 2
    shapes = [(3 * (d_slab + f_slab), cols) for _ in range(blocks)]
    shapes[1] = (shapes[1][0] + blocks * rows * (wide // cols), cols)
    return pl.pallas_call(
        functools.partial(pack_kernel, wide),
        grid=(1,),
        in_specs=[SMEM, whole(weight.shape), whole(fast.shape), whole(output.shape)],
        out_specs=[whole(s) for s in shapes],
        out_shape=[jax.ShapeDtypeStruct(s, BF16) for s in shapes],
        cost_estimate=cost(0, 2 * 2**20),
        compiler_params=LIMIT,
        name="pack",
    )(ids, weight, fast, output)


def prepare_kernel(count, d_slab, f_slab, heads, dim, outs, o_rows, o_parts, ids_ref, *refs):
    slabs, refs = refs[:count], refs[count:]
    w_ref, ft_ref = refs[:2]
    f_all = refs[-1]
    units = count * f_slab
    cols = heads * dim
    for k in range(count):
        source = ids_ref[0] ^ k
        for j in range(3):
            w_ref[pl.ds(pl.multiple_of(source * d_slab, d_slab), d_slab), j * cols : (j + 1) * cols] = slabs[k][
                j * d_slab : (j + 1) * d_slab
            ]
            f_all[j, pl.ds(pl.multiple_of(source * f_slab, f_slab), f_slab)] = slabs[k][
                3 * d_slab + j * f_slab : 3 * d_slab + (j + 1) * f_slab
            ]
        at = 3 * (d_slab + f_slab)
        for b in range(outs):
            for c in range(o_parts):
                place = b * count * o_rows + source * o_rows
                refs[2][pl.ds(pl.multiple_of(place, o_rows), o_rows), c * cols : (c + 1) * cols] = slabs[k][
                    at : at + o_rows
                ]
                at += o_rows
    blank = jnp.zeros((units, dim), BF16)
    for j in range(3):
        for h in range(heads):
            part = f_all[j, :, h * dim : (h + 1) * dim]
            ft_ref[h, j] = jnp.concatenate([blank, part] if j == 2 else [part, blank], axis=1)


def prepare(ids, slabs, d_slab, f_slab, heads, dim, outs=0, o_rows=0, o_parts=0):
    count = len(slabs)
    cols = heads * dim
    depth, units = count * d_slab, count * f_slab
    shapes = [(depth, 3 * cols), (heads, 3, units, 2 * dim)]
    if outs:
        shapes.append((outs * count * o_rows, o_parts * cols))
    return pl.pallas_call(
        functools.partial(prepare_kernel, count, d_slab, f_slab, heads, dim, outs, o_rows, o_parts),
        grid=(1,),
        in_specs=[SMEM] + [whole(s.shape) for s in slabs],
        out_specs=[whole(s) for s in shapes],
        out_shape=[jax.ShapeDtypeStruct(s, BF16) for s in shapes],
        scratch_shapes=[pltpu.VMEM((3, units, cols), BF16)],
        cost_estimate=cost(0, 8 * 2**20),
        compiler_params=LIMIT,
        name="prepare",
    )(ids, *slabs)


def front_kernel(heads, dim, chunks, steps, base, tokens, last, ids_ref, mask_ref, w_ref, ft_ref, *refs):
    x_refs, refs = refs[:chunks], refs[chunks:]
    if last:
        prev_ref, refs = refs[0], refs[4:]
        slots = refs[3 : 3 + heads]
        turn_ref = refs[-1]
    else:
        grad_ref = refs[3]
    q_ref, k_ref, v_ref = refs[:3]
    acc_ref, flip_ref, both_ref = refs[3 + heads : 6 + heads] if last else refs[4:7]
    step = pl.program_id(0)
    tile = q_ref.shape[0]
    cols = heads * dim
    units = ft_ref.shape[2]

    @pl.when(step == 0)
    def _():
        acc_ref[...] = jnp.zeros_like(acc_ref)

    x = x_refs[0][...]
    for c in range(1, chunks):
        x = jnp.where(step >= c * steps, x_refs[c][...], x)
    packed = mm(x, w_ref[...], 1, 0).astype(BF16)
    place = ((base + step // steps) ^ ids_ref[1]) * tokens + (step % steps) * tile
    mask = -(mask_ref[:, pl.ds(pl.multiple_of(place, tile), tile)].astype(F32))
    mask = jnp.broadcast_to(mask, (8, tile)).T[:, :1]
    side = lax.broadcasted_iota(jnp.int32, (cols, cols), 0) // dim
    same = side == lax.broadcasted_iota(jnp.int32, (cols, cols), 1) // dim
    spread = jnp.where(same, 1.0 / dim, 0.0).astype(BF16)

    def norm(part):
        part = part.astype(F32)
        return (part * lax.rsqrt(mm((part * part).astype(BF16), spread, 1, 0) + 1e-05)).astype(BF16)

    q_ref[...] = norm(packed[:, :cols])
    keys = norm(packed[:, cols : 2 * cols])
    values = packed[:, 2 * cols :]
    targets = (values.astype(F32) * mask).astype(BF16)
    ones = jnp.ones((tile, dim), BF16)
    for h in range(heads):
        rows = slice(h * dim, (h + 1) * dim)
        v_ref[h] = jnp.concatenate([values[:, rows], ones], axis=1)
        both = jnp.concatenate([keys[:, rows], targets[:, rows]], axis=1)
        flip_ref[h] = both
        both = both.T
        both_ref[h] = both
        k_ref[rows] = both[:dim]
    width = min(FRONT_WIDTH, units)

    def gradient(h, carry):
        both, flip = both_ref[h], flip_ref[h]
        for c in range(0, units, width):
            part = slice(c, c + width)
            first = mm(ft_ref[h, 0, part], both, 1, 0).astype(FRONT_TYPE)
            third = mm(ft_ref[h, 1, part], both, 1, 0).astype(FRONT_TYPE)
            back = mm(ft_ref[h, 2, part], both, 1, 0).astype(FRONT_TYPE)
            sigma = sigmoid(first)
            silu = first * sigma
            hidden = (silu * third).astype(BF16)
            d_third = (back * silu).astype(BF16)
            d_first = (back * third * (sigma + silu * (1.0 - sigma))).astype(BF16)
            acc_ref[h, 0, part] += mm(d_first, flip, 1, 0)
            acc_ref[h, 1, part] += mm(d_third, flip, 1, 0)
            acc_ref[h, 2, part] += mm(hidden, flip, 1, 0)
        return carry

    lax.fori_loop(0, heads, gradient, 0, unroll=FRONT_UNROLL)

    @pl.when(step == pl.num_programs(0) - 1)
    def _():
        def finish(h, carry):
            for j in range(3):
                rows = slice(j * dim, (j + 1) * dim)
                total = acc_ref[h, j].T[dim if j == 2 else 0 :][:dim]
                if last:
                    slot = h ^ lax.rem(ids_ref[0] >> 1, heads)
                    turn_ref[slot, rows] = (total + prev_ref[h, rows]).astype(BF16)
                else:
                    grad_ref[h, rows] = total
            return carry

        lax.fori_loop(0, heads, finish, 0)
        if last:
            for i in range(heads):
                slots[i][...] = turn_ref[i]


def front(ids, xs, base, wt, ft, mask, parts, before=None):
    tokens, depth = xs[0].shape
    heads, _, units, dim = ft.shape
    dim //= 2
    cols = heads * dim
    tile = min(FRONT_TILE, tokens)
    steps = tokens // tile
    chunks = len(xs)
    total = parts * tokens
    first = base * steps
    last = before is not None

    def pick(c):
        return lambda i: (jnp.clip(i - c * steps, 0, steps - 1), 0)

    in_specs = [SMEM, whole(mask.shape), whole(wt.shape), whole(ft.shape)]
    in_specs += [pl.BlockSpec((tile, depth), pick(c)) for c in range(chunks)]
    out_specs = [
        pl.BlockSpec((tile, cols), lambda i: (first + i, 0)),
        pl.BlockSpec((cols, tile), lambda i: (0, first + i)),
        pl.BlockSpec((heads, tile, 2 * dim), lambda i: (0, first + i, 0)),
    ]
    out_shape = [
        jax.ShapeDtypeStruct((total, cols), BF16),
        jax.ShapeDtypeStruct((cols, total), BF16),
        jax.ShapeDtypeStruct((heads, total, 2 * dim), BF16),
    ]
    args = [ids, mask, wt, ft, *xs]
    scratch = [
        pltpu.VMEM((heads, 3, units, 2 * dim), F32),
        pltpu.VMEM((heads, tile, 2 * dim), BF16),
        pltpu.VMEM((heads, 2 * dim, tile), BF16),
    ]
    aliases = {}
    if last:
        in_specs += [whole(before[3].shape)] + [ANY] * 3
        aliases = {len(args) + 1 + i: i for i in range(3)}
        args += [before[3], *before[:3]]
        out_specs += [whole((3 * dim, units))] * heads
        out_shape += [jax.ShapeDtypeStruct((3 * dim, units), BF16)] * heads
        scratch.append(pltpu.VMEM((heads, 3 * dim, units), BF16))
    else:
        out_specs.append(whole((heads, 3 * dim, units)))
        out_shape.append(jax.ShapeDtypeStruct((heads, 3 * dim, units), F32))
    here = chunks * tokens
    return pl.pallas_call(
        functools.partial(front_kernel, heads, dim, chunks, steps, base, tokens, last),
        grid=(chunks * steps,),
        in_specs=in_specs,
        out_specs=out_specs,
        out_shape=out_shape,
        scratch_shapes=scratch,
        input_output_aliases=aliases,
        cost_estimate=cost(4 * here * cols * 2 * (3 * depth + 6 * units), 6 * 2**20),
        compiler_params=LIMIT,
        name="front",
    )(*args)


def attend_kernel(heads, dim, q_ref, k_ref, v_ref, *refs):
    o_ref = refs[-1]
    span = k_ref.shape[1]
    width = min(ATTEND_WIDTH, span)

    def pair(p, carry):
        at = pl.ds(pl.multiple_of(p * 2 * dim, 2 * dim), 2 * dim)
        both = q_ref[:, at]
        keys = k_ref[at]
        outs = []
        for i in range(2):
            total = None
            for c in range(0, span, width):
                scores = mm(both[:, i * dim : (i + 1) * dim], keys[i * dim : (i + 1) * dim, c : c + width], 1, 0)
                probs = jnp.exp2(scores * (score_scale * log2_e)).astype(BF16)
                part = mm(probs, v_ref[2 * p + i, c : c + width], 1, 0)
                total = part if total is None else total + part
            outs.append(total[:, :dim] / total[:, dim:])
        o_ref[:, at] = jnp.concatenate(outs, axis=1).astype(BF16)
        return carry

    lax.fori_loop(0, heads // 2, pair, 0, unroll=ATTEND_UNROLL)


def attend(q, k, v, start, count, before=None):
    total, cols = q.shape
    heads, _, twice = v.shape
    tile = min(ATTEND_TILE, count)
    first = start // tile
    extra = [] if before is None else [before]
    return pl.pallas_call(
        functools.partial(attend_kernel, heads, twice // 2),
        grid=(count // tile,),
        in_specs=[pl.BlockSpec((tile, cols), lambda i: (first + i, 0)), whole(k.shape), whole(v.shape)]
        + [ANY] * len(extra),
        out_specs=pl.BlockSpec((tile, cols), lambda i: (first + i, 0)),
        out_shape=jax.ShapeDtypeStruct((total, cols), BF16),
        input_output_aliases={3: 0} if extra else {},
        cost_estimate=cost(4 * 4 * count * total * cols, 4 * 2**20),
        compiler_params=LIMIT,
        name="attend",
    )(q, k, v, *extra)


def split(x):
    high = x.astype(BF16)
    return high, (x - high.astype(F32)).astype(BF16)


def mm_split(a, b, ca, cb):
    return mm(a[0], b[0], ca, cb) + (mm(a[0], b[1], ca, cb) + mm(a[1], b[0], ca, cb))


def newton_kernel(ids_ref, ft_ref, own_ref, got_ref, o_ref):
    dim = ft_ref.shape[3] // 2
    summed = own_ref[...].astype(F32) + got_ref[...].astype(F32)
    scaled = []
    for j in range(3):
        total = summed[j * dim : (j + 1) * dim]
        scaled.append(total * lax.rsqrt(jnp.sum(total * total, keepdims=True) + 1e-06))
    current = jnp.concatenate(scaled, axis=0)
    side = lax.broadcasted_iota(jnp.int32, (3 * dim, 3 * dim), 0) // dim
    same = side == lax.broadcasted_iota(jnp.int32, (3 * dim, 3 * dim), 1) // dim

    halves = split(current)
    cross = mm(halves[0], halves[1], 1, 1)
    gram = jnp.where(same, mm(halves[0], halves[0], 1, 1) + (cross + cross.T), 0.0)
    eye = lax.broadcasted_iota(jnp.int32, gram.shape, 0) == lax.broadcasted_iota(jnp.int32, gram.shape, 1)
    identity = jnp.where(eye, 1.0, 0.0)

    def advance(_, state):
        gram, factor = state
        parts = split(gram)
        squared = mm_split(parts, parts, 1, 0)
        polynomial = newton_coeffs[0] * identity + newton_coeffs[1] * gram + newton_coeffs[2] * squared
        step = split(polynomial)
        factor = mm_split(step, split(factor), 1, 0)
        gram = mm_split(step, split(mm_split(parts, step, 1, 0)), 1, 0)
        return gram, factor

    _, factor = lax.fori_loop(0, NS_STEPS, advance, (gram, identity))
    current = mm_split(split(factor), halves, 1, 0)
    for j in range(3):
        rows = slice(j * dim, (j + 1) * dim)
        initial = ft_ref[0, j].astype(F32).T[dim if j == 2 else 0 :][:dim]
        o_ref[rows] = (initial - learn_rate * current[rows]).astype(BF16)


def newton(ids, ft, own, got):
    heads, _, units, twice = ft.shape
    fixed = lambda i, ids: (0, 0)
    return pl.pallas_call(
        newton_kernel,
        grid_spec=pltpu.PrefetchScalarGridSpec(
            num_scalar_prefetch=1,
            grid=(1,),
            in_specs=[
                pl.BlockSpec((1, 3, units, twice), lambda i, ids: (lax.rem(ids[0] >> 1, heads), 0, 0, 0)),
                pl.BlockSpec(own.shape, fixed),
                pl.BlockSpec(got.shape, fixed),
            ],
            out_specs=pl.BlockSpec(own.shape, fixed),
        ),
        out_shape=jax.ShapeDtypeStruct(own.shape, BF16),
        cost_estimate=cost(2**30, 2 * 2**20),
        compiler_params=LIMIT,
        name="newton",
    )(ids, ft, own, got)


def apply_kernel(heads, dim, group, stage, first_k, count, ids_ref, q_ref, a_ref, *refs):
    early_ref, refs = (refs[0], refs[1:]) if stage == "late" else (None, refs)
    units_refs, o_refs, fast_ref = refs[:count], refs[count:-1], refs[-1]
    step = pl.program_id(0)
    place = ids_ref[0] >> 1
    mine = lax.rem(place, heads) // group
    side = 1 - mine if stage == "late" else mine
    span = group * dim
    if stage == "all":
        at = slice(None)
    else:
        at = pl.ds(pl.multiple_of(side * span, span), span)

    @pl.when(step == 0)
    def _():
        for k in range(count):
            head = place ^ (first_k + k)
            if stage != "all":
                fast_ref[lax.rem(head, group)] = units_refs[k][...]
                continue

            @pl.when(head < heads)
            def _():
                fast_ref[head] = units_refs[k][...]

    queries = q_ref[:, at]
    outs = []
    for h in range(group):
        query = queries[:, h * dim : (h + 1) * dim]
        first = mm(query, fast_ref[h, :dim], 1, 0).astype(APPLY_TYPE)
        third = mm(query, fast_ref[h, dim : 2 * dim], 1, 0).astype(APPLY_TYPE)
        hidden = (first * sigmoid(first) * third).astype(BF16)
        outs.append(unit(mm(hidden, fast_ref[h, 2 * dim :], 1, 1), 1))
    mixed = (jnp.concatenate(outs, axis=1) + a_ref[:, at].astype(F32)).astype(BF16)
    if stage == "early":
        o_refs[0][...] = mixed
        return
    steps = o_refs[0].shape[0] // mixed.shape[0]
    for c, o_ref in enumerate(o_refs):

        @pl.when(step // steps == c)
        def _():
            rows = pl.ds(pl.multiple_of((step % steps) * mixed.shape[0], mixed.shape[0]), mixed.shape[0])
            if stage == "late":
                o_ref[rows, at] = mixed
                o_ref[rows, pl.ds(pl.multiple_of(mine * span, span), span)] = early_ref[...]
            else:
                o_ref[rows] = mixed


def apply_fast(ids, q, attended, fast, heads, stage, tokens, start, chunks, early=None):
    total, cols = q.shape
    dim = cols // heads
    units = fast[0].shape[1]
    group = heads if stage == "all" else heads // 2
    first_k = 0
    if stage != "all":
        first_k = 0 if stage == "early" else group
        fast = fast[first_k : first_k + group]
    tile = min(APPLY_TILE, tokens)
    first = start // tile
    rows = pl.BlockSpec((tile, cols), lambda i: (first + i, 0))
    args, in_specs = [ids, q, attended], [SMEM, rows, rows]
    if stage == "late":
        args.append(early)
        in_specs.append(pl.BlockSpec((tile, group * dim), lambda i: (first + i, 0)))
    if stage == "early":
        out_specs = pl.BlockSpec((tile, group * dim), lambda i: (first + i, 0))
        out_shape = jax.ShapeDtypeStruct((total, group * dim), BF16)
    else:
        out_specs = [whole((tokens, cols))] * chunks
        out_shape = [jax.ShapeDtypeStruct((tokens, cols), BF16)] * chunks
    here = chunks * tokens
    return pl.pallas_call(
        functools.partial(apply_kernel, heads, dim, group, stage, first_k, len(fast)),
        grid=(here // tile,),
        in_specs=in_specs + [whole(a.shape) for a in fast],
        out_specs=out_specs,
        out_shape=out_shape,
        scratch_shapes=[pltpu.VMEM((group, 3 * dim, units), BF16)],
        cost_estimate=cost(4 * 2 * here * group * dim * units * 3, 2 * 2**20),
        compiler_params=LIMIT,
    )(*args, *fast)


def project_kernel(count, more, ids_ref, s_ref, own_ref, pair_ref, *refs):
    parts, outs = refs[:count], refs[count:]
    cols = parts[0].shape[1]
    half = own_ref.shape[1]
    low = ids_ref[1] & 1
    for which, w_ref in ((low, own_ref), (1 - low, pair_ref)):
        projected = None
        for k in range(count):
            place = pl.multiple_of((ids_ref[1] ^ k) * cols, cols)
            part = mm(parts[k][...], w_ref[pl.ds(place, cols)], 1, 0)
            projected = part if projected is None else projected + part
        here = pl.ds(pl.multiple_of(which * half, half), half)
        outs[0][:, here] = (s_ref[:, here].astype(F32) + projected).astype(BF16)
    if more:
        outs[1][...] = unit(outs[0][...].astype(F32), 1).astype(BF16)


def project(ids, stream, own, pair, layer, parts, more):
    tokens, depth = stream.shape
    tile = min(256, tokens)
    cols = parts[0].shape[1]
    count = 2 if more else 1
    weight = pl.BlockSpec((depth, own.shape[1]), lambda i: (layer, 0))
    return pl.pallas_call(
        functools.partial(project_kernel, len(parts), more),
        grid=(tokens // tile,),
        in_specs=[SMEM, pl.BlockSpec((tile, depth), lambda i: (i, 0)), weight, weight]
        + [pl.BlockSpec((tile, cols), lambda i: (i, 0))] * len(parts),
        out_specs=[pl.BlockSpec((tile, depth), lambda i: (i, 0))] * count,
        out_shape=[jax.ShapeDtypeStruct((tokens, depth), BF16)] * count,
        cost_estimate=cost(2 * tokens * depth * depth, 6 * 2**20),
        compiler_params=LIMIT,
        name="project",
    )(ids, stream, own, pair, *parts)


def solution(mesh):
    views, parts = mesh.shape["view"], mesh.shape["head"]

    def swap(x, axis, k, keep=None):
        pairs = [(i, i ^ k) for i in range(mesh.shape[axis])]
        if keep is not None:
            pairs = [p for p in pairs if keep(*p)]
        return lax.ppermute(x, axis, pairs)

    def gather_view(block):
        slabs = {0: block}
        for k in range(2, views, 2):
            slabs[k] = swap(block, "view", k)
        for k in range(0, views, 2):
            slabs[k + 1] = swap(slabs[k], "view", 1)
        return [slabs[k] for k in range(views)]

    def shards(features, attend_weight, output_weight, fast_init, update_mask):
        blocks, _, d_slab, cols = attend_weight.shape
        heads, dim, f_slab = fast_init.shape[1], fast_init.shape[3], fast_init.shape[4]
        tokens = features.shape[0]
        half = parts // 2
        staged = views // 2 == heads and heads % 4 == 0
        ids = jnp.stack([lax.axis_index("view"), lax.axis_index("head")]).astype(jnp.int32)
        o_rows, o_parts = output_weight.shape[1], output_weight.shape[2] // 2 // cols
        payloads = pack(ids, attend_weight, fast_init, output_weight)

        stream = features
        normed = unit(features.astype(F32), 1).astype(BF16)
        for layer in range(blocks):
            xs = [normed]
            for k in range(1, parts):
                high = 1 << (k.bit_length() - 1)
                from_k, hop = (0, k) if high == k else (high, k ^ high)
                xs.append(swap(xs[from_k], "head", hop))
            if layer == 0:
                slabs = gather_view(payloads[0])
                wt, ft = prepare(ids, slabs, d_slab, f_slab, heads, dim)
                later = []
                for b, block in enumerate(payloads[1:], 1):
                    slabs = gather_view(block)
                    shape = (blocks, o_rows, o_parts) if b == 1 else ()
                    later.append(prepare(ids, slabs, d_slab, f_slab, heads, dim, *shape))
                out_own = later[0][2]
                out_pair = swap(out_own, "head", 1)
            else:
                wt, ft = later[layer - 1][:2]
            front_a = front(ids, xs[:half], 0, wt, ft, update_mask, parts)
            q, k, v, *grads = front(ids, xs[half:], half, wt, ft, update_mask, parts, front_a)
            near = grads[0].astype(F32)
            for i in range(1, views // 2):
                part = swap(grads[i % heads], "view", 2 * i, lambda _, o: (o >> 1) < heads)
                near = near + part.astype(F32)
            near = near.astype(BF16)
            got = swap(near, "view", 1)
            count = half * tokens
            attended = None
            least = count // 2
            for start, n in ((least, 2 * count - least), (0, least)):
                attended = attend(q, k, v, start, n, attended)
            fresh = newton(ids, ft, near, got)
            fast = [fresh] + [swap(fresh, "view", 2 * i, lambda i, o: (i >> 1) < heads) for i in range(1, views // 2)]
            stage, early = "all", None
            if staged:
                stage = "late"
                early = apply_fast(ids, q, attended, fast, heads, "early", tokens, 0, parts)
            mixed_b = apply_fast(ids, q, attended, fast, heads, stage, tokens, count, half, early)
            mixed_a = apply_fast(ids, q, attended, fast, heads, stage, tokens, 0, half, early)
            mixed = [*mixed_a, *mixed_b]
            received = [mixed[0]] + [swap(mixed[i], "head", i) for i in range(1, parts)]
            more = layer + 1 < blocks
            result = project(ids, stream, out_own, out_pair, layer, received, more)
            stream = result[0]
            normed = result[-1]
        return stream


    return jax.shard_map(
        shards,
        mesh=mesh,
        in_specs=(
            P(("view", "head"), None),
            P(None, None, "view", "head"),
            P(None, "view", None),
            P(None, "head", None, None, "view"),
            P("view", None),
        ),
        out_specs=P(("view", "head"), None),
        check_vma=False,
    )
```

```python
import functools
import math

import jax
import jax.numpy as jnp
from jax import lax
from jax.experimental import pallas as pl
from jax.experimental.pallas import tpu as pltpu
from jax.sharding import PartitionSpec as P


NS_STEPS = 5

newton_coeffs = (3.4445, -4.775, 2.0315)
learn_rate = 1.0
score_scale = 0.25
log2_e = math.log2(math.e)

F32, BF16 = jnp.float32, jnp.bfloat16
SMEM = pl.BlockSpec(memory_space=pltpu.SMEM)

FRONT_TILE, FRONT_WIDTH, FRONT_UNROLL, FRONT_TYPE = 256, 512, 4, F32
APPLY_TILE, APPLY_TYPE = 256, F32
VMEM_MIB = 32
ATTEND_TILE, ATTEND_WIDTH, ATTEND_UNROLL = 256, 1024, False


def mm(a, b, ca, cb, precision=None):
    return lax.dot_general(
        a, b, (((ca,), (cb,)), ((), ())), preferred_element_type=F32, precision=precision
    )


def whole(shape):
    return pl.BlockSpec(tuple(shape), lambda i: (0,) * len(shape))


def cost(flops, nbytes, trans=0):
    return pl.CostEstimate(flops=int(flops), bytes_accessed=int(nbytes), transcendentals=int(trans))


def sigmoid(x):
    return 0.5 * jnp.tanh(0.5 * x) + 0.5


def unit(part, axis):
    return part * lax.rsqrt(jnp.mean(part * part, axis=axis, keepdims=True) + 1e-05)


LIMIT = pltpu.CompilerParams(vmem_limit_bytes=VMEM_MIB * 2**20)
ANY = pl.BlockSpec(memory_space=pl.ANY)


def pack_kernel(outs, wide, *refs):
    w_ref, f_ref, p_ref = refs[-3 - (outs > 0)], refs[-2 - (outs > 0)], refs[-1]
    _, _, d_slab, cols = w_ref.shape
    heads, f_slab = f_ref.shape[1], f_ref.shape[4]
    at = 3 * d_slab
    for j in range(3):
        p_ref[j * d_slab : (j + 1) * d_slab] = w_ref[0, j]
        parts = [f_ref[0, h, j].astype(F32).T for h in range(heads)]
        p_ref[at : at + f_slab] = jnp.concatenate(parts, axis=1).astype(BF16)
        at += f_slab
    if not outs:
        return
    ids_ref, o_ref = refs[0], refs[3]
    rows = o_ref.shape[1]
    for i in range(outs):
        for c in range(0, wide, cols):
            place = pl.multiple_of((ids_ref[1] & 1) * wide + c, cols)
            p_ref[at : at + rows] = o_ref[i, :, pl.ds(place, cols)]
            at += rows


def pack(block, weight, fast, ids=None, output=None):
    _, _, d_slab, cols = weight.shape
    rows, outs, wide = 3 * (d_slab + fast.shape[4]), 0, 0
    args = [weight, fast]
    in_specs = [pl.BlockSpec((1, *a.shape[1:]), lambda i, n=a.ndim: (block,) + (0,) * (n - 1)) for a in args]
    if output is not None:
        outs, wide = output.shape[0], output.shape[2] // 2
        rows += outs * output.shape[1] * (wide // cols)
        args = [ids, *args, output]
        in_specs = [SMEM, *in_specs, whole(output.shape)]
    return pl.pallas_call(
        functools.partial(pack_kernel, outs, wide),
        grid=(1,),
        in_specs=in_specs,
        out_specs=whole((rows, cols)),
        out_shape=jax.ShapeDtypeStruct((rows, cols), BF16),
        cost_estimate=cost(0, 2 * 2**20),
        name="pack",
    )(*args)


def prepare_kernel(count, d_slab, f_slab, heads, dim, outs, o_rows, o_parts, ids_ref, *refs):
    slabs, refs = refs[:count], refs[count:]
    w_ref, ft_ref = refs[:2]
    f_all = refs[-1]
    units = count * f_slab
    cols = heads * dim
    for k in range(count):
        source = ids_ref[0] ^ k
        for j in range(3):
            w_ref[pl.ds(pl.multiple_of(source * d_slab, d_slab), d_slab), j * cols : (j + 1) * cols] = slabs[k][
                j * d_slab : (j + 1) * d_slab
            ]
            f_all[j, pl.ds(pl.multiple_of(source * f_slab, f_slab), f_slab)] = slabs[k][
                3 * d_slab + j * f_slab : 3 * d_slab + (j + 1) * f_slab
            ]
        at = 3 * (d_slab + f_slab)
        for b in range(outs):
            for c in range(o_parts):
                place = b * count * o_rows + source * o_rows
                refs[2][pl.ds(pl.multiple_of(place, o_rows), o_rows), c * cols : (c + 1) * cols] = slabs[k][
                    at : at + o_rows
                ]
                at += o_rows
    blank = jnp.zeros((units, dim), BF16)
    for j in range(3):
        for h in range(heads):
            part = f_all[j, :, h * dim : (h + 1) * dim]
            ft_ref[h, j] = jnp.concatenate([blank, part] if j == 2 else [part, blank], axis=1)


def prepare(ids, slabs, d_slab, f_slab, heads, dim, outs=0, o_rows=0, o_parts=0):
    count = len(slabs)
    cols = heads * dim
    depth, units = count * d_slab, count * f_slab
    shapes = [(depth, 3 * cols), (heads, 3, units, 2 * dim)]
    if outs:
        shapes.append((outs * count * o_rows, o_parts * cols))
    return pl.pallas_call(
        functools.partial(prepare_kernel, count, d_slab, f_slab, heads, dim, outs, o_rows, o_parts),
        grid=(1,),
        in_specs=[SMEM] + [whole(s.shape) for s in slabs],
        out_specs=[whole(s) for s in shapes],
        out_shape=[jax.ShapeDtypeStruct(s, BF16) for s in shapes],
        scratch_shapes=[pltpu.VMEM((3, units, cols), BF16)],
        cost_estimate=cost(0, 8 * 2**20),
        compiler_params=LIMIT,
        name="prepare",
    )(ids, *slabs)


def front_kernel(heads, dim, chunks, steps, base, offset, tokens, more, last, ids_ref, mask_ref, w_ref, ft_ref, *refs):
    x_refs, refs = refs[:chunks], refs[chunks:]
    if more:
        prev_ref, refs = refs[0], refs[4:]
    if last:
        slots = refs[3 : 3 + heads]
        turn_ref = refs[-1]
    else:
        grad_ref = refs[3]
    q_ref, k_ref, v_ref = refs[:3]
    acc_ref, flip_ref, both_ref = refs[3 + heads : 6 + heads] if last else refs[4:7]
    step = pl.program_id(0)
    tile = q_ref.shape[0]
    cols = heads * dim
    units = ft_ref.shape[2]

    @pl.when(step == 0)
    def _():
        acc_ref[...] = jnp.zeros_like(acc_ref)

    x = x_refs[0][...]
    for c in range(1, chunks):
        x = jnp.where(step >= c * steps, x_refs[c][...], x)
    packed = mm(x, w_ref[...], 1, 0).astype(BF16)
    place = ((base + step // steps) ^ ids_ref[1]) * tokens + offset + (step % steps) * tile
    mask = -(mask_ref[:, pl.ds(pl.multiple_of(place, tile), tile)].astype(F32))
    mask = jnp.broadcast_to(mask, (8, tile)).T[:, :1]
    side = lax.broadcasted_iota(jnp.int32, (cols, cols), 0) // dim
    same = side == lax.broadcasted_iota(jnp.int32, (cols, cols), 1) // dim
    spread = jnp.where(same, 1.0 / dim, 0.0).astype(BF16)

    def norm(part):
        part = part.astype(F32)
        return (part * lax.rsqrt(mm((part * part).astype(BF16), spread, 1, 0) + 1e-05)).astype(BF16)

    q_ref[...] = norm(packed[:, :cols])
    keys = norm(packed[:, cols : 2 * cols])
    values = packed[:, 2 * cols :]
    targets = (values.astype(F32) * mask).astype(BF16)
    ones = jnp.ones((tile, dim), BF16)
    for h in range(heads):
        rows = slice(h * dim, (h + 1) * dim)
        v_ref[h] = jnp.concatenate([values[:, rows], ones], axis=1)
        both = jnp.concatenate([keys[:, rows], targets[:, rows]], axis=1)
        flip_ref[h] = both
        both = both.T
        both_ref[h] = both
        k_ref[rows] = both[:dim]
    width = min(FRONT_WIDTH, units)

    def gradient(h, carry):
        both, flip = both_ref[h], flip_ref[h]
        for c in range(0, units, width):
            part = slice(c, c + width)
            first = mm(ft_ref[h, 0, part], both, 1, 0).astype(FRONT_TYPE)
            third = mm(ft_ref[h, 1, part], both, 1, 0).astype(FRONT_TYPE)
            back = mm(ft_ref[h, 2, part], both, 1, 0).astype(FRONT_TYPE)
            sigma = sigmoid(first)
            silu = first * sigma
            hidden = (silu * third).astype(BF16)
            d_third = (back * silu).astype(BF16)
            d_first = (back * third * (sigma + silu * (1.0 - sigma))).astype(BF16)
            acc_ref[h, 0, part] += mm(d_first, flip, 1, 0)
            acc_ref[h, 1, part] += mm(d_third, flip, 1, 0)
            acc_ref[h, 2, part] += mm(hidden, flip, 1, 0)
        return carry

    lax.fori_loop(0, heads, gradient, 0, unroll=FRONT_UNROLL)

    @pl.when(step == pl.num_programs(0) - 1)
    def _():
        def finish(h, carry):
            for j in range(3):
                rows = slice(j * dim, (j + 1) * dim)
                total = acc_ref[h, j].T[dim if j == 2 else 0 :][:dim]
                if more:
                    total += prev_ref[h, rows]
                if last:
                    slot = h ^ lax.rem(ids_ref[0] >> 1, heads)
                    turn_ref[slot, rows] = total.astype(BF16)
                else:
                    grad_ref[h, rows] = total
            return carry

        lax.fori_loop(0, heads, finish, 0)
        if last:
            for i in range(heads):
                slots[i][...] = turn_ref[i]


def front(ids, xs, base, offset, tokens, wt, ft, mask, parts, before=None, last=False):
    rows, depth = xs[0].shape
    heads, _, units, dim = ft.shape
    dim //= 2
    cols = heads * dim
    tile = min(FRONT_TILE, rows)
    steps = rows // tile
    chunks = len(xs)
    total = parts * tokens
    more = before is not None

    def block(i):
        return (base + i // steps) * (tokens // tile) + offset // tile + i % steps

    def pick(c):
        return lambda i: (jnp.clip(i - c * steps, 0, steps - 1), 0)

    in_specs = [SMEM, whole(mask.shape), whole(wt.shape), whole(ft.shape)]
    in_specs += [pl.BlockSpec((tile, depth), pick(c)) for c in range(chunks)]
    out_specs = [
        pl.BlockSpec((tile, cols), lambda i: (block(i), 0)),
        pl.BlockSpec((cols, tile), lambda i: (0, block(i))),
        pl.BlockSpec((heads, tile, 2 * dim), lambda i: (0, block(i), 0)),
    ]
    out_shape = [
        jax.ShapeDtypeStruct((total, cols), BF16),
        jax.ShapeDtypeStruct((cols, total), BF16),
        jax.ShapeDtypeStruct((heads, total, 2 * dim), BF16),
    ]
    args = [ids, mask, wt, ft, *xs]
    scratch = [
        pltpu.VMEM((heads, 3, units, 2 * dim), F32),
        pltpu.VMEM((heads, tile, 2 * dim), BF16),
        pltpu.VMEM((heads, 2 * dim, tile), BF16),
    ]
    aliases = {}
    if more:
        in_specs += [whole(before[3].shape)] + [ANY] * 3
        aliases = {len(args) + 1 + i: i for i in range(3)}
        args += [before[3], *before[:3]]
    if last:
        out_specs += [whole((3 * dim, units))] * heads
        out_shape += [jax.ShapeDtypeStruct((3 * dim, units), BF16)] * heads
        scratch.append(pltpu.VMEM((heads, 3 * dim, units), BF16))
    else:
        out_specs.append(whole((heads, 3 * dim, units)))
        out_shape.append(jax.ShapeDtypeStruct((heads, 3 * dim, units), F32))
    here = chunks * rows
    return pl.pallas_call(
        functools.partial(front_kernel, heads, dim, chunks, steps, base, offset, tokens, more, last),
        grid=(chunks * steps,),
        in_specs=in_specs,
        out_specs=out_specs,
        out_shape=out_shape,
        scratch_shapes=scratch,
        input_output_aliases=aliases,
        cost_estimate=cost(4 * here * cols * 2 * (3 * depth + 6 * units), 6 * 2**20),
        compiler_params=LIMIT,
        name="front",
    )(*args)


def attend_kernel(heads, dim, q_ref, k_ref, v_ref, *refs):
    o_ref = refs[-1]
    span = k_ref.shape[1]
    width = min(ATTEND_WIDTH, span)

    def pair(p, carry):
        at = pl.ds(pl.multiple_of(p * 2 * dim, 2 * dim), 2 * dim)
        both = q_ref[:, at]
        keys = k_ref[at]
        outs = []
        for i in range(2):
            total = None
            for c in range(0, span, width):
                scores = mm(both[:, i * dim : (i + 1) * dim], keys[i * dim : (i + 1) * dim, c : c + width], 1, 0)
                probs = jnp.exp2(scores * (score_scale * log2_e)).astype(BF16)
                part = mm(probs, v_ref[2 * p + i, c : c + width], 1, 0)
                total = part if total is None else total + part
            outs.append(total[:, :dim] / total[:, dim:])
        o_ref[:, at] = jnp.concatenate(outs, axis=1).astype(BF16)
        return carry

    lax.fori_loop(0, heads // 2, pair, 0, unroll=ATTEND_UNROLL)


def attend(q, k, v, start, count, before=None):
    total, cols = q.shape
    heads, _, twice = v.shape
    tile = min(ATTEND_TILE, count)
    first = start // tile
    extra = [] if before is None else [before]
    return pl.pallas_call(
        functools.partial(attend_kernel, heads, twice // 2),
        grid=(count // tile,),
        in_specs=[pl.BlockSpec((tile, cols), lambda i: (first + i, 0)), whole(k.shape), whole(v.shape)]
        + [ANY] * len(extra),
        out_specs=pl.BlockSpec((tile, cols), lambda i: (first + i, 0)),
        out_shape=jax.ShapeDtypeStruct((total, cols), BF16),
        input_output_aliases={3: 0} if extra else {},
        cost_estimate=cost(4 * 4 * count * total * cols, 4 * 2**20),
        compiler_params=LIMIT,
        name="attend",
    )(q, k, v, *extra)


def split(x):
    high = x.astype(BF16)
    return high, (x - high.astype(F32)).astype(BF16)


def mm_split(a, b, ca, cb):
    return mm(a[0], b[0], ca, cb) + (mm(a[0], b[1], ca, cb) + mm(a[1], b[0], ca, cb))


def newton_kernel(ids_ref, ft_ref, own_ref, got_ref, o_ref):
    dim = ft_ref.shape[3] // 2
    summed = own_ref[...].astype(F32) + got_ref[...].astype(F32)
    scaled = []
    for j in range(3):
        total = summed[j * dim : (j + 1) * dim]
        scaled.append(total * lax.rsqrt(jnp.sum(total * total, keepdims=True) + 1e-06))
    current = jnp.concatenate(scaled, axis=0)
    side = lax.broadcasted_iota(jnp.int32, (3 * dim, 3 * dim), 0) // dim
    same = side == lax.broadcasted_iota(jnp.int32, (3 * dim, 3 * dim), 1) // dim

    halves = split(current)
    cross = mm(halves[0], halves[1], 1, 1)
    gram = jnp.where(same, mm(halves[0], halves[0], 1, 1) + (cross + cross.T), 0.0)
    eye = lax.broadcasted_iota(jnp.int32, gram.shape, 0) == lax.broadcasted_iota(jnp.int32, gram.shape, 1)
    identity = jnp.where(eye, 1.0, 0.0)

    def polynomial(gram, parts):
        squared = mm_split(parts, parts, 1, 0)
        return newton_coeffs[0] * identity + newton_coeffs[1] * gram + newton_coeffs[2] * squared

    def advance(_, state):
        gram, factor = state
        parts = split(gram)
        step = split(polynomial(gram, parts))
        factor = mm_split(step, split(factor), 1, 0)
        gram = mm_split(step, split(mm_split(parts, step, 1, 0)), 1, 0)
        return gram, factor

    gram, factor = lax.fori_loop(0, NS_STEPS - 1, advance, (gram, identity))
    factor = mm_split(split(polynomial(gram, split(gram))), split(factor), 1, 0)
    current = mm_split(split(factor), halves, 1, 0)
    for j in range(3):
        rows = slice(j * dim, (j + 1) * dim)
        initial = ft_ref[0, j].astype(F32).T[dim if j == 2 else 0 :][:dim]
        o_ref[rows] = (initial - learn_rate * current[rows]).astype(BF16)


def newton(ids, ft, own, got):
    heads, _, units, twice = ft.shape
    fixed = lambda i, ids: (0, 0)
    return pl.pallas_call(
        newton_kernel,
        grid_spec=pltpu.PrefetchScalarGridSpec(
            num_scalar_prefetch=1,
            grid=(1,),
            in_specs=[
                pl.BlockSpec((1, 3, units, twice), lambda i, ids: (lax.rem(ids[0] >> 1, heads), 0, 0, 0)),
                pl.BlockSpec(own.shape, fixed),
                pl.BlockSpec(got.shape, fixed),
            ],
            out_specs=pl.BlockSpec(own.shape, fixed),
        ),
        out_shape=jax.ShapeDtypeStruct(own.shape, BF16),
        cost_estimate=cost(2**30, 2 * 2**20),
        compiler_params=LIMIT,
        name="newton",
    )(ids, ft, own, got)


def apply_kernel(heads, dim, group, stage, first_k, count, merge, tokens, spans, ids_ref, q_ref, a_ref, *refs):
    early_ref, refs = (refs[0], refs[1:]) if merge else (None, refs)
    units_refs, o_refs, fast_ref = refs[:count], refs[count:-1], refs[-1]
    step = pl.program_id(0)
    place = ids_ref[0] >> 1
    mine = lax.rem(place, heads) // group
    side = 1 - mine if stage == "late" else mine
    span = group * dim
    if stage == "all":
        at = slice(None)
    else:
        at = pl.ds(pl.multiple_of(side * span, span), span)

    @pl.when(step == 0)
    def _():
        for k in range(count):
            head = place ^ (first_k + k)
            if stage != "all":
                fast_ref[lax.rem(head, group)] = units_refs[k][...]
                continue

            @pl.when(head < heads)
            def _():
                fast_ref[head] = units_refs[k][...]

    queries = q_ref[:, at]
    outs = []
    for h in range(group):
        query = queries[:, h * dim : (h + 1) * dim]
        first = mm(query, fast_ref[h, :dim], 1, 0).astype(APPLY_TYPE)
        third = mm(query, fast_ref[h, dim : 2 * dim], 1, 0).astype(APPLY_TYPE)
        hidden = (first * sigmoid(first) * third).astype(BF16)
        outs.append(unit(mm(hidden, fast_ref[h, 2 * dim :], 1, 1), 1))
    mixed = (jnp.concatenate(outs, axis=1) + a_ref[:, at].astype(F32)).astype(BF16)
    tile = mixed.shape[0]
    steps = tokens // tile
    for (chunk, chunks), o_ref in zip(spans, o_refs):

        @pl.when((step >= chunk * steps) & (step < (chunk + chunks) * steps))
        def _():
            rows = pl.ds(pl.multiple_of((step - chunk * steps) * tile, tile), tile)
            if early_ref is None:
                o_ref[rows] = mixed
            else:
                o_ref[rows, at] = mixed
                o_ref[rows, pl.ds(pl.multiple_of(mine * span, span), span)] = early_ref[...]


def apply_fast(ids, q, attended, fast, heads, stage, tokens, base, spans, early=None):
    cols = q.shape[1]
    dim = cols // heads
    units = fast[0].shape[1]
    group, first_k = heads, 0
    if stage != "all":
        group = heads // 2
        first_k = 0 if stage == "early" else group
        fast = fast[first_k : first_k + group]
    tile = min(APPLY_TILE, tokens)
    first = base * tokens // tile
    rows = pl.BlockSpec((tile, cols), lambda i: (first + i, 0))
    args, in_specs = [ids, q, attended], [SMEM, rows, rows]
    merge = early is not None
    if merge:
        args.append(early)
        in_specs.append(pl.BlockSpec((tile, group * dim), lambda i: (first + i, 0)))
    width = cols if merge or stage == "all" else group * dim
    shapes = [(chunks * tokens, width) for _, chunks in spans]
    here = sum(chunks for _, chunks in spans) * tokens
    return pl.pallas_call(
        functools.partial(
            apply_kernel, heads, dim, group, stage, first_k, len(fast), merge, tokens, tuple(spans)
        ),
        grid=(here // tile,),
        in_specs=in_specs + [whole(a.shape) for a in fast],
        out_specs=[whole(shape) for shape in shapes],
        out_shape=[jax.ShapeDtypeStruct(shape, BF16) for shape in shapes],
        scratch_shapes=[pltpu.VMEM((group, 3 * dim, units), BF16)],
        cost_estimate=cost(4 * 2 * here * group * dim * units * 3, 2 * 2**20),
        compiler_params=LIMIT,
    )(*args, *fast)


def project_kernel(heads, dim, places, more, ids_ref, s_ref, own_ref, pair_ref, *refs):
    count = len(places)
    parts, outs = refs[:count], refs[count:]
    cols = heads * dim
    group = max(heads // 2, 1)
    mine = lax.rem(ids_ref[0] >> 1, heads) // group
    half = own_ref.shape[1]
    low = ids_ref[1] & 1
    for which, w_ref in ((low, own_ref), (1 - low, pair_ref)):
        projected = None
        for (k, late), part_ref in zip(places, parts):
            place, wide = (ids_ref[1] ^ k) * cols, part_ref.shape[1]
            if late is not None:
                place += (1 - mine if late else mine) * wide
            part = mm(part_ref[...], w_ref[pl.ds(pl.multiple_of(place, wide), wide)], 1, 0)
            projected = part if projected is None else projected + part
        here = pl.ds(pl.multiple_of(which * half, half), half)
        outs[0][:, here] = (s_ref[:, here].astype(F32) + projected).astype(BF16)
    if not more:
        return
    normed = unit(outs[0][...].astype(F32), 1).astype(BF16)
    outs[1][...] = normed
    for c in range(2):

        @pl.when(pl.program_id(0) == c)
        def _():
            outs[2 + c][...] = normed


def project(ids, stream, own, pair, layer, parts, places, heads, dim, more):
    tokens, depth = stream.shape
    tile = tokens // 2
    weight = pl.BlockSpec((depth, own.shape[1]), lambda i: (layer, 0))
    rows = pl.BlockSpec((tile, depth), lambda i: (i, 0))
    out_specs = [rows] + ([rows] + [whole((tile, depth))] * 2 if more else [])
    sizes = [tokens] + ([tokens, tile, tile] if more else [])
    return pl.pallas_call(
        functools.partial(project_kernel, heads, dim, tuple(places), more),
        grid=(2,),
        in_specs=[SMEM, rows, weight, weight] + [pl.BlockSpec((tile, p.shape[1]), lambda i: (i, 0)) for p in parts],
        out_specs=out_specs,
        out_shape=[jax.ShapeDtypeStruct((n, depth), BF16) for n in sizes],
        cost_estimate=cost(2 * tokens * depth * depth, 6 * 2**20),
        compiler_params=LIMIT,
        name="project",
    )(ids, stream, own, pair, *parts)


def solution(mesh):
    views, parts = mesh.shape["view"], mesh.shape["head"]

    def swap(x, axis, k, keep=None):
        pairs = [(i, i ^ k) for i in range(mesh.shape[axis])]
        if keep is not None:
            pairs = [p for p in pairs if keep(*p)]
        return lax.ppermute(x, axis, pairs)

    def gather_view(block):
        slabs = {0: block}
        for k in range(2, views, 2):
            slabs[k] = swap(block, "view", k)
        for k in range(0, views, 2):
            slabs[k + 1] = swap(slabs[k], "view", 1)
        return [slabs[k] for k in range(views)]

    def shards(features, attend_weight, output_weight, fast_init, update_mask):
        blocks, _, d_slab, cols = attend_weight.shape
        heads, dim, f_slab = fast_init.shape[1], fast_init.shape[3], fast_init.shape[4]
        tokens = features.shape[0]
        half = parts // 2
        staged = views // 2 == heads and heads % 4 == 0
        ids = jnp.stack([lax.axis_index("view"), lax.axis_index("head")]).astype(jnp.int32)
        o_rows, o_parts = output_weight.shape[1], output_weight.shape[2] // 2 // cols
        payloads = []
        for b in range(blocks):
            payloads.append(pack(b, attend_weight, fast_init, *((ids, output_weight) if b == 1 else ())))

        stream = features
        normed = unit(features.astype(F32), 1).astype(BF16)
        for layer in range(blocks):
            pieces = halves if layer else [normed]
            near_xs, far_xs = [normed], [[p] for p in pieces]
            for k in range(1, half):
                high = 1 << (k.bit_length() - 1)
                from_k, hop = (0, k) if high == k else (high, k ^ high)
                near_xs.append(swap(near_xs[from_k], "head", hop))
            for far in far_xs:
                far[0] = swap(far[0], "head", half)
                for k in range(1, half):
                    far.append(swap(far[0], "head", k))
            if layer == 0:
                slabs = gather_view(payloads[0])
                wt, ft = prepare(ids, slabs, d_slab, f_slab, heads, dim)
                later = []
                for b, block in enumerate(payloads[1:], 1):
                    slabs = gather_view(block)
                    shape = (blocks, o_rows, o_parts) if b == 1 else ()
                    later.append(prepare(ids, slabs, d_slab, f_slab, heads, dim, *shape))
                out_own = later[0][2]
                out_pair = swap(out_own, "head", 1)
            else:
                wt, ft = later[layer - 1][:2]
            state = front(ids, near_xs, 0, 0, tokens, wt, ft, update_mask, parts)
            for p, far in enumerate(far_xs):
                offset = p * far[0].shape[0]
                final = p + 1 == len(far_xs)
                state = front(ids, far, half, offset, tokens, wt, ft, update_mask, parts, state, final)
            q, k, v, *grads = state
            near = grads[0].astype(F32)
            for i in range(1, views // 2):
                part = swap(grads[i % heads], "view", 2 * i, lambda _, o: (o >> 1) < heads)
                near = near + part.astype(F32)
            near = near.astype(BF16)
            got = swap(near, "view", 1)
            count = half * tokens
            attended = None
            least = count // 2
            for start, n in ((least, 2 * count - least), (0, least)):
                attended = attend(q, k, v, start, n, attended)
            fresh = newton(ids, ft, near, got)
            fast = [fresh] + [swap(fresh, "view", 2 * i, lambda i, o: (i >> 1) < heads) for i in range(1, views // 2)]
            received, places = [], []
            far_chunks = [(c, 1) for c in range(half)]
            if staged:
                spans = [(0, half)] + [(c, 1) for c in range(half, parts)]
                early, *sent = apply_fast(ids, q, attended, fast, heads, "early", tokens, 0, spans)
                for i, x in enumerate(sent, half):
                    received.append(swap(x, "head", i))
                    places.append((i, 0))
                sent = apply_fast(ids, q, attended, fast, heads, "late", tokens, half, far_chunks)
                for i, x in enumerate(sent, half):
                    received.append(swap(x, "head", i))
                    places.append((i, 1))
                mixed = apply_fast(ids, q, attended, fast, heads, "late", tokens, 0, far_chunks, early)
            else:
                sent = apply_fast(ids, q, attended, fast, heads, "all", tokens, half, far_chunks)
                for i, x in enumerate(sent, half):
                    received.append(swap(x, "head", i))
                    places.append((i, None))
                mixed = apply_fast(ids, q, attended, fast, heads, "all", tokens, 0, far_chunks)
            near_parts = [x if i == 0 else swap(x, "head", i) for i, x in enumerate(mixed)]
            received = near_parts + received
            places = [(i, None) for i in range(half)] + places
            more = layer + 1 < blocks
            result = project(ids, stream, out_own, out_pair, layer, received, places, heads, dim, more)
            stream = result[0]
            if more:
                normed, *halves = result[1:]
        return stream


    return jax.shard_map(
        shards,
        mesh=mesh,
        in_specs=(
            P(("view", "head"), None),
            P(None, None, "view", "head"),
            P(None, "view", None),
            P(None, "head", None, None, "view"),
            P("view", None),
        ),
        out_specs=P(("view", "head"), None),
        check_vma=False,
    )
```

```python
import functools
import math

import jax
import jax.numpy as jnp
from jax import lax
from jax.experimental import pallas as pl
from jax.experimental.pallas import tpu as pltpu
from jax.sharding import PartitionSpec as P


NS_STEPS = 5

newton_coeffs = (3.4445, -4.775, 2.0315)
learn_rate = 1.0
score_scale = 0.25
log2_e = math.log2(math.e)

F32, BF16 = jnp.float32, jnp.bfloat16
VIEW, HEAD = "view", "head"
EARLY, LATE, ALL = "early", "late", "all"


SMEM = pl.BlockSpec(memory_space=pltpu.SMEM)

FRONT_TILE, FRONT_WIDTH, FRONT_UNROLL, FRONT_TYPE = 256, 512, 4, F32
APPLY_TILE, APPLY_TYPE = 256, F32
VMEM_MIB = 32
ATTEND_TILE, ATTEND_WIDTH, ATTEND_UNROLL = 256, 1024, False


def mm(a, b, ca, cb, precision=None):
    return lax.dot_general(
        a, b, (((ca,), (cb,)), ((), ())), preferred_element_type=F32, precision=precision
    )


def whole(shape):
    return pl.BlockSpec(tuple(shape), lambda i: (0,) * len(shape))


def cost(flops, nbytes, trans=0):
    return pl.CostEstimate(flops=int(flops), bytes_accessed=int(nbytes), transcendentals=int(trans))


def sigmoid(x):
    return 0.5 * jnp.tanh(0.5 * x) + 0.5


def unit(part, axis):
    return part * lax.rsqrt(jnp.mean(part * part, axis=axis, keepdims=True) + 1e-05)


LIMIT = pltpu.CompilerParams(vmem_limit_bytes=VMEM_MIB * 2**20)
ANY = pl.BlockSpec(memory_space=pl.ANY)


def pack_kernel(outs, wide, *refs):
    w_ref, f_ref, p_ref = refs[-3 - (outs > 0)], refs[-2 - (outs > 0)], refs[-1]
    _, _, d_slab, cols = w_ref.shape
    heads, f_slab = f_ref.shape[1], f_ref.shape[4]
    at = 3 * d_slab
    for j in range(3):
        p_ref[j * d_slab : (j + 1) * d_slab] = w_ref[0, j]
        parts = [f_ref[0, h, j].astype(F32).T for h in range(heads)]
        p_ref[at : at + f_slab] = jnp.concatenate(parts, axis=1).astype(BF16)
        at += f_slab
    if not outs:
        return
    ids_ref, o_ref = refs[0], refs[3]
    rows = o_ref.shape[1]
    for i in range(outs):
        for c in range(0, wide, cols):
            place = pl.multiple_of((ids_ref[1] & 1) * wide + c, cols)
            p_ref[at : at + rows] = o_ref[i, :, pl.ds(place, cols)]
            at += rows


def pack(block, weight, fast, ids=None, output=None):
    _, _, d_slab, cols = weight.shape
    rows, outs, wide = 3 * (d_slab + fast.shape[4]), 0, 0
    args = [weight, fast]
    in_specs = [pl.BlockSpec((1, *a.shape[1:]), lambda i, n=a.ndim: (block,) + (0,) * (n - 1)) for a in args]
    if output is not None:
        outs, wide = output.shape[0], output.shape[2] // 2
        rows += outs * output.shape[1] * (wide // cols)
        args = [ids, *args, output]
        in_specs = [SMEM, *in_specs, whole(output.shape)]
    return pl.pallas_call(
        functools.partial(pack_kernel, outs, wide),
        grid=(1,),
        in_specs=in_specs,
        out_specs=whole((rows, cols)),
        out_shape=jax.ShapeDtypeStruct((rows, cols), BF16),
        cost_estimate=cost(0, 2 * 2**20),
        name="pack",
    )(*args)


def prepare_kernel(count, d_slab, f_slab, heads, dim, outs, o_rows, o_parts, ids_ref, *refs):
    slabs, refs = refs[:count], refs[count:]
    w_ref, ft_ref = refs[:2]
    f_all = refs[-1]
    units = count * f_slab
    cols = heads * dim
    for k in range(count):
        source = ids_ref[0] ^ k
        for j in range(3):
            w_ref[pl.ds(pl.multiple_of(source * d_slab, d_slab), d_slab), j * cols : (j + 1) * cols] = slabs[k][
                j * d_slab : (j + 1) * d_slab
            ]
            f_all[j, pl.ds(pl.multiple_of(source * f_slab, f_slab), f_slab)] = slabs[k][
                3 * d_slab + j * f_slab : 3 * d_slab + (j + 1) * f_slab
            ]
        at = 3 * (d_slab + f_slab)
        for b in range(outs):
            for c in range(o_parts):
                place = b * count * o_rows + source * o_rows
                refs[2][pl.ds(pl.multiple_of(place, o_rows), o_rows), c * cols : (c + 1) * cols] = slabs[k][
                    at : at + o_rows
                ]
                at += o_rows
    blank = jnp.zeros((units, dim), BF16)
    for j in range(3):
        for h in range(heads):
            part = f_all[j, :, h * dim : (h + 1) * dim]
            ft_ref[h, j] = jnp.concatenate([blank, part] if j == 2 else [part, blank], axis=1)


def prepare(ids, slabs, d_slab, f_slab, heads, dim, outs=0, o_rows=0, o_parts=0):
    count = len(slabs)
    cols = heads * dim
    depth, units = count * d_slab, count * f_slab
    shapes = [(depth, 3 * cols), (heads, 3, units, 2 * dim)]
    if outs:
        shapes.append((outs * count * o_rows, o_parts * cols))
    return pl.pallas_call(
        functools.partial(prepare_kernel, count, d_slab, f_slab, heads, dim, outs, o_rows, o_parts),
        grid=(1,),
        in_specs=[SMEM] + [whole(s.shape) for s in slabs],
        out_specs=[whole(s) for s in shapes],
        out_shape=[jax.ShapeDtypeStruct(s, BF16) for s in shapes],
        scratch_shapes=[pltpu.VMEM((3, units, cols), BF16)],
        cost_estimate=cost(0, 8 * 2**20),
        compiler_params=LIMIT,
        name="prepare",
    )(ids, *slabs)


def front_kernel(heads, dim, chunks, steps, base, offset, tokens, more, last, ids_ref, mask_ref, w_ref, ft_ref, *refs):
    x_refs, refs = refs[:chunks], refs[chunks:]
    if more:
        prev_ref, refs = refs[0], refs[4:]
    if last:
        slots = refs[3 : 3 + heads]
        turn_ref = refs[-1]
    else:
        grad_ref = refs[3]
    q_ref, k_ref, v_ref = refs[:3]
    acc_ref, flip_ref, both_ref = refs[3 + heads : 6 + heads] if last else refs[4:7]
    step = pl.program_id(0)
    tile = q_ref.shape[0]
    cols = heads * dim
    units = ft_ref.shape[2]

    @pl.when(step == 0)
    def _():
        acc_ref[...] = jnp.zeros_like(acc_ref)

    x = x_refs[0][...]
    for c in range(1, chunks):
        x = jnp.where(step >= c * steps, x_refs[c][...], x)
    packed = mm(x, w_ref[...], 1, 0).astype(BF16)
    place = ((base + step // steps) ^ ids_ref[1]) * tokens + offset + (step % steps) * tile
    mask = -(mask_ref[:, pl.ds(pl.multiple_of(place, tile), tile)].astype(F32))
    mask = jnp.broadcast_to(mask, (8, tile)).T[:, :1]
    side = lax.broadcasted_iota(jnp.int32, (cols, cols), 0) // dim
    same = side == lax.broadcasted_iota(jnp.int32, (cols, cols), 1) // dim
    spread = jnp.where(same, 1.0 / dim, 0.0).astype(BF16)

    def norm(part):
        part = part.astype(F32)
        return (part * lax.rsqrt(mm((part * part).astype(BF16), spread, 1, 0) + 1e-05)).astype(BF16)

    q_ref[...] = norm(packed[:, :cols])
    keys = norm(packed[:, cols : 2 * cols])
    values = packed[:, 2 * cols :]
    targets = (values.astype(F32) * mask).astype(BF16)
    ones = jnp.ones((tile, dim), BF16)
    for h in range(heads):
        rows = slice(h * dim, (h + 1) * dim)
        v_ref[h] = jnp.concatenate([values[:, rows], ones], axis=1)
        both = jnp.concatenate([keys[:, rows], targets[:, rows]], axis=1)
        flip_ref[h] = both
        both = both.T
        both_ref[h] = both
        k_ref[rows] = both[:dim]
    width = min(FRONT_WIDTH, units)

    def gradient(h, carry):
        both, flip = both_ref[h], flip_ref[h]
        for c in range(0, units, width):
            part = slice(c, c + width)
            first = mm(ft_ref[h, 0, part], both, 1, 0).astype(FRONT_TYPE)
            third = mm(ft_ref[h, 1, part], both, 1, 0).astype(FRONT_TYPE)
            back = mm(ft_ref[h, 2, part], both, 1, 0).astype(FRONT_TYPE)
            sigma = sigmoid(first)
            silu = first * sigma
            hidden = (silu * third).astype(BF16)
            d_third = (back * silu).astype(BF16)
            d_first = (back * third * (sigma + silu * (1.0 - sigma))).astype(BF16)
            acc_ref[h, 0, part] += mm(d_first, flip, 1, 0)
            acc_ref[h, 1, part] += mm(d_third, flip, 1, 0)
            acc_ref[h, 2, part] += mm(hidden, flip, 1, 0)
        return carry

    lax.fori_loop(0, heads, gradient, 0, unroll=FRONT_UNROLL)

    @pl.when(step == pl.num_programs(0) - 1)
    def _():
        def finish(h, carry):
            for j in range(3):
                rows = slice(j * dim, (j + 1) * dim)
                total = acc_ref[h, j].T[dim if j == 2 else 0 :][:dim]
                if more:
                    total += prev_ref[h, rows]
                if last:
                    slot = h ^ lax.rem(ids_ref[0] >> 1, heads)
                    turn_ref[slot, rows] = total.astype(BF16)
                else:
                    grad_ref[h, rows] = total
            return carry

        lax.fori_loop(0, heads, finish, 0)
        if last:
            for i in range(heads):
                slots[i][...] = turn_ref[i]


def front(ids, xs, base, offset, tokens, wt, ft, mask, parts, before=None, last=False):
    rows, depth = xs[0].shape
    heads, _, units, dim = ft.shape
    dim //= 2
    cols = heads * dim
    tile = min(FRONT_TILE, rows)
    steps = rows // tile
    chunks = len(xs)
    total = parts * tokens
    more = before is not None

    def block(i):
        return (base + i // steps) * (tokens // tile) + offset // tile + i % steps

    def pick(c):
        return lambda i: (jnp.clip(i - c * steps, 0, steps - 1), 0)

    in_specs = [SMEM, whole(mask.shape), whole(wt.shape), whole(ft.shape)]
    in_specs += [pl.BlockSpec((tile, depth), pick(c)) for c in range(chunks)]
    out_specs = [
        pl.BlockSpec((tile, cols), lambda i: (block(i), 0)),
        pl.BlockSpec((cols, tile), lambda i: (0, block(i))),
        pl.BlockSpec((heads, tile, 2 * dim), lambda i: (0, block(i), 0)),
    ]
    out_shape = [
        jax.ShapeDtypeStruct((total, cols), BF16),
        jax.ShapeDtypeStruct((cols, total), BF16),
        jax.ShapeDtypeStruct((heads, total, 2 * dim), BF16),
    ]
    args = [ids, mask, wt, ft, *xs]
    scratch = [
        pltpu.VMEM((heads, 3, units, 2 * dim), F32),
        pltpu.VMEM((heads, tile, 2 * dim), BF16),
        pltpu.VMEM((heads, 2 * dim, tile), BF16),
    ]
    aliases = {}
    if more:
        in_specs += [whole(before[3].shape)] + [ANY] * 3
        aliases = {len(args) + 1 + i: i for i in range(3)}
        args += [before[3], *before[:3]]
    if last:
        out_specs += [whole((3 * dim, units))] * heads
        out_shape += [jax.ShapeDtypeStruct((3 * dim, units), BF16)] * heads
        scratch.append(pltpu.VMEM((heads, 3 * dim, units), BF16))
    else:
        out_specs.append(whole((heads, 3 * dim, units)))
        out_shape.append(jax.ShapeDtypeStruct((heads, 3 * dim, units), F32))
    here = chunks * rows
    return pl.pallas_call(
        functools.partial(front_kernel, heads, dim, chunks, steps, base, offset, tokens, more, last),
        grid=(chunks * steps,),
        in_specs=in_specs,
        out_specs=out_specs,
        out_shape=out_shape,
        scratch_shapes=scratch,
        input_output_aliases=aliases,
        cost_estimate=cost(4 * here * cols * 2 * (3 * depth + 6 * units), 6 * 2**20),
        compiler_params=LIMIT,
        name="front",
    )(*args)


def attend_kernel(heads, dim, q_ref, k_ref, v_ref, *refs):
    o_ref = refs[-1]
    span = k_ref.shape[1]
    width = min(ATTEND_WIDTH, span)

    def pair(p, carry):
        at = pl.ds(pl.multiple_of(p * 2 * dim, 2 * dim), 2 * dim)
        both = q_ref[:, at]
        keys = k_ref[at]
        outs = []
        for i in range(2):
            total = None
            for c in range(0, span, width):
                scores = mm(both[:, i * dim : (i + 1) * dim], keys[i * dim : (i + 1) * dim, c : c + width], 1, 0)
                probs = jnp.exp2(scores * (score_scale * log2_e)).astype(BF16)
                part = mm(probs, v_ref[2 * p + i, c : c + width], 1, 0)
                total = part if total is None else total + part
            outs.append(total[:, :dim] / total[:, dim:])
        o_ref[:, at] = jnp.concatenate(outs, axis=1).astype(BF16)
        return carry

    lax.fori_loop(0, heads // 2, pair, 0, unroll=ATTEND_UNROLL)


def attend(q, k, v, start, count, before=None):
    total, cols = q.shape
    heads, _, twice = v.shape
    tile = min(ATTEND_TILE, count)
    first = start // tile
    extra = [] if before is None else [before]
    return pl.pallas_call(
        functools.partial(attend_kernel, heads, twice // 2),
        grid=(count // tile,),
        in_specs=[pl.BlockSpec((tile, cols), lambda i: (first + i, 0)), whole(k.shape), whole(v.shape)]
        + [ANY] * len(extra),
        out_specs=pl.BlockSpec((tile, cols), lambda i: (first + i, 0)),
        out_shape=jax.ShapeDtypeStruct((total, cols), BF16),
        input_output_aliases={3: 0} if extra else {},
        cost_estimate=cost(4 * 4 * count * total * cols, 4 * 2**20),
        compiler_params=LIMIT,
        name="attend",
    )(q, k, v, *extra)


def split(x):
    high = x.astype(BF16)
    return high, (x - high.astype(F32)).astype(BF16)


def mm_split(a, b, ca, cb):
    return mm(a[0], b[0], ca, cb) + (mm(a[0], b[1], ca, cb) + mm(a[1], b[0], ca, cb))


def newton_kernel(ids_ref, ft_ref, own_ref, got_ref, o_ref):
    dim = ft_ref.shape[3] // 2
    summed = own_ref[...].astype(F32) + got_ref[...].astype(F32)
    scaled = []
    for j in range(3):
        total = summed[j * dim : (j + 1) * dim]
        scaled.append(total * lax.rsqrt(jnp.sum(total * total, keepdims=True) + 1e-06))
    current = jnp.concatenate(scaled, axis=0)
    side = lax.broadcasted_iota(jnp.int32, (3 * dim, 3 * dim), 0) // dim
    same = side == lax.broadcasted_iota(jnp.int32, (3 * dim, 3 * dim), 1) // dim

    halves = split(current)
    cross = mm(halves[0], halves[1], 1, 1)
    gram = jnp.where(same, mm(halves[0], halves[0], 1, 1) + (cross + cross.T), 0.0)
    eye = lax.broadcasted_iota(jnp.int32, gram.shape, 0) == lax.broadcasted_iota(jnp.int32, gram.shape, 1)
    identity = jnp.where(eye, 1.0, 0.0)

    def polynomial(gram, parts):
        squared = mm_split(parts, parts, 1, 0)
        return newton_coeffs[0] * identity + newton_coeffs[1] * gram + newton_coeffs[2] * squared

    def advance(_, state):
        gram, factor = state
        parts = split(gram)
        step = split(polynomial(gram, parts))
        factor = mm_split(step, split(factor), 1, 0)
        gram = mm_split(step, split(mm_split(parts, step, 1, 0)), 1, 0)
        return gram, factor

    gram, factor = lax.fori_loop(0, NS_STEPS - 1, advance, (gram, identity))
    factor = mm_split(split(polynomial(gram, split(gram))), split(factor), 1, 0)
    current = mm_split(split(factor), halves, 1, 0)
    for j in range(3):
        rows = slice(j * dim, (j + 1) * dim)
        initial = ft_ref[0, j].astype(F32).T[dim if j == 2 else 0 :][:dim]
        o_ref[rows] = (initial - learn_rate * current[rows]).astype(BF16)


def newton(ids, ft, own, got):
    heads, _, units, twice = ft.shape
    fixed = lambda i, ids: (0, 0)
    return pl.pallas_call(
        newton_kernel,
        grid_spec=pltpu.PrefetchScalarGridSpec(
            num_scalar_prefetch=1,
            grid=(1,),
            in_specs=[
                pl.BlockSpec((1, 3, units, twice), lambda i, ids: (lax.rem(ids[0] >> 1, heads), 0, 0, 0)),
                pl.BlockSpec(own.shape, fixed),
                pl.BlockSpec(got.shape, fixed),
            ],
            out_specs=pl.BlockSpec(own.shape, fixed),
        ),
        out_shape=jax.ShapeDtypeStruct(own.shape, BF16),
        cost_estimate=cost(2**30, 2 * 2**20),
        compiler_params=LIMIT,
        name="newton",
    )(ids, ft, own, got)


def apply_kernel(heads, dim, group, stage, first_k, count, merge, tokens, spans, ids_ref, q_ref, a_ref, *refs):
    early_ref, refs = (refs[0], refs[1:]) if merge else (None, refs)
    units_refs, o_refs, fast_ref = refs[:count], refs[count:-1], refs[-1]
    step = pl.program_id(0)
    place = ids_ref[0] >> 1
    mine = lax.rem(place, heads) // group
    side = 1 - mine if stage == LATE else mine
    span = group * dim
    if stage == ALL:
        at = slice(None)
    else:
        at = pl.ds(pl.multiple_of(side * span, span), span)

    @pl.when(step == 0)
    def _():
        for k in range(count):
            head = place ^ (first_k + k)
            if stage != ALL:
                fast_ref[lax.rem(head, group)] = units_refs[k][...]
                continue

            @pl.when(head < heads)
            def _():
                fast_ref[head] = units_refs[k][...]

    queries = q_ref[:, at]
    outs = []
    for h in range(group):
        query = queries[:, h * dim : (h + 1) * dim]
        first = mm(query, fast_ref[h, :dim], 1, 0).astype(APPLY_TYPE)
        third = mm(query, fast_ref[h, dim : 2 * dim], 1, 0).astype(APPLY_TYPE)
        hidden = (first * sigmoid(first) * third).astype(BF16)
        outs.append(unit(mm(hidden, fast_ref[h, 2 * dim :], 1, 1), 1))
    mixed = (jnp.concatenate(outs, axis=1) + a_ref[:, at].astype(F32)).astype(BF16)
    tile = mixed.shape[0]
    steps = tokens // tile
    for (chunk, chunks), o_ref in zip(spans, o_refs):

        @pl.when((step >= chunk * steps) & (step < (chunk + chunks) * steps))
        def _():
            rows = pl.ds(pl.multiple_of((step - chunk * steps) * tile, tile), tile)
            if early_ref is None:
                o_ref[rows] = mixed
            else:
                o_ref[rows, at] = mixed
                o_ref[rows, pl.ds(pl.multiple_of(mine * span, span), span)] = early_ref[...]


def apply_fast(ids, q, attended, fast, heads, stage, tokens, base, spans, early=None):
    cols = q.shape[1]
    dim = cols // heads
    units = fast[0].shape[1]
    group, first_k = heads, 0
    if stage != ALL:
        group = heads // 2
        first_k = 0 if stage == EARLY else group
        fast = fast[first_k : first_k + group]
    tile = min(APPLY_TILE, tokens)
    first = base * tokens // tile
    rows = pl.BlockSpec((tile, cols), lambda i: (first + i, 0))
    args, in_specs = [ids, q, attended], [SMEM, rows, rows]
    merge = early is not None
    if merge:
        args.append(early)
        in_specs.append(pl.BlockSpec((tile, group * dim), lambda i: (first + i, 0)))
    width = cols if merge or stage == ALL else group * dim
    shapes = [(chunks * tokens, width) for _, chunks in spans]
    here = sum(chunks for _, chunks in spans) * tokens
    return pl.pallas_call(
        functools.partial(
            apply_kernel, heads, dim, group, stage, first_k, len(fast), merge, tokens, tuple(spans)
        ),
        grid=(here // tile,),
        in_specs=in_specs + [whole(a.shape) for a in fast],
        out_specs=[whole(shape) for shape in shapes],
        out_shape=[jax.ShapeDtypeStruct(shape, BF16) for shape in shapes],
        scratch_shapes=[pltpu.VMEM((group, 3 * dim, units), BF16)],
        cost_estimate=cost(4 * 2 * here * group * dim * units * 3, 2 * 2**20),
        compiler_params=LIMIT,
    )(*args, *fast)


def project_kernel(heads, dim, places, more, ids_ref, s_ref, own_ref, pair_ref, *refs):
    count = len(places)
    parts, outs = refs[:count], refs[count:]
    cols = heads * dim
    group = max(heads // 2, 1)
    mine = lax.rem(ids_ref[0] >> 1, heads) // group
    half = own_ref.shape[1]
    low = ids_ref[1] & 1
    for which, w_ref in ((low, own_ref), (1 - low, pair_ref)):
        projected = None
        for (k, late), part_ref in zip(places, parts):
            place, wide = (ids_ref[1] ^ k) * cols, part_ref.shape[1]
            if late is not None:
                place += (1 - mine if late else mine) * wide
            part = mm(part_ref[...], w_ref[pl.ds(pl.multiple_of(place, wide), wide)], 1, 0)
            projected = part if projected is None else projected + part
        here = pl.ds(pl.multiple_of(which * half, half), half)
        outs[0][:, here] = (s_ref[:, here].astype(F32) + projected).astype(BF16)
    if not more:
        return
    normed = unit(outs[0][...].astype(F32), 1).astype(BF16)
    outs[1][...] = normed
    for c in range(2):

        @pl.when(pl.program_id(0) == c)
        def _():
            outs[2 + c][...] = normed


def project(ids, stream, own, pair, layer, parts, places, heads, dim, more):
    tokens, depth = stream.shape
    tile = tokens // 2
    weight = pl.BlockSpec((depth, own.shape[1]), lambda i: (layer, 0))
    rows = pl.BlockSpec((tile, depth), lambda i: (i, 0))
    out_specs = [rows] + ([rows] + [whole((tile, depth))] * 2 if more else [])
    sizes = [tokens] + ([tokens, tile, tile] if more else [])
    return pl.pallas_call(
        functools.partial(project_kernel, heads, dim, tuple(places), more),
        grid=(2,),
        in_specs=[SMEM, rows, weight, weight] + [pl.BlockSpec((tile, p.shape[1]), lambda i: (i, 0)) for p in parts],
        out_specs=out_specs,
        out_shape=[jax.ShapeDtypeStruct((n, depth), BF16) for n in sizes],
        cost_estimate=cost(2 * tokens * depth * depth, 6 * 2**20),
        compiler_params=LIMIT,
        name="project",
    )(ids, stream, own, pair, *parts)


def solution(mesh):
    views, parts = mesh.shape[VIEW], mesh.shape[HEAD]

    def swap(x, axis, k, keep=None):
        pairs = [(i, i ^ k) for i in range(mesh.shape[axis])]
        if keep is not None:
            pairs = [p for p in pairs if keep(*p)]
        return lax.ppermute(x, axis, pairs)

    def gather_view(block):
        slabs = {0: block}
        for k in range(2, views, 2):
            slabs[k] = swap(block, VIEW, k)
        for k in range(0, views, 2):
            slabs[k + 1] = swap(slabs[k], VIEW, 1)
        return [slabs[k] for k in range(views)]

    def shards(features, attend_weight, output_weight, fast_init, update_mask):
        blocks, _, d_slab, cols = attend_weight.shape
        heads, dim, f_slab = fast_init.shape[1], fast_init.shape[3], fast_init.shape[4]
        tokens = features.shape[0]
        half = parts // 2
        staged = views // 2 == heads and heads % 4 == 0
        ids = jnp.stack([lax.axis_index(VIEW), lax.axis_index(HEAD)]).astype(jnp.int32)
        o_rows, o_parts = output_weight.shape[1], output_weight.shape[2] // 2 // cols
        payloads = []
        for b in range(blocks):
            payloads.append(pack(b, attend_weight, fast_init, *((ids, output_weight) if b == 1 else ())))

        stream = features
        normed = unit(features.astype(F32), 1).astype(BF16)
        for layer in range(blocks):
            pieces = halves if layer else [normed]
            near_xs, far_xs = [normed], [[p] for p in pieces]
            for k in range(1, half):
                high = 1 << (k.bit_length() - 1)
                from_k, hop = (0, k) if high == k else (high, k ^ high)
                near_xs.append(swap(near_xs[from_k], HEAD, hop))
            for far in far_xs:
                far[0] = swap(far[0], HEAD, half)
                for k in range(1, half):
                    far.append(swap(far[0], HEAD, k))
            if layer == 0:
                slabs = gather_view(payloads[0])
                wt, ft = prepare(ids, slabs, d_slab, f_slab, heads, dim)
                later = []
                for b, block in enumerate(payloads[1:], 1):
                    slabs = gather_view(block)
                    shape = (blocks, o_rows, o_parts) if b == 1 else ()
                    later.append(prepare(ids, slabs, d_slab, f_slab, heads, dim, *shape))
                out_own = later[0][2]
                out_pair = swap(out_own, HEAD, 1)
            else:
                wt, ft = later[layer - 1][:2]
            state = front(ids, near_xs, 0, 0, tokens, wt, ft, update_mask, parts)
            for p, far in enumerate(far_xs):
                offset = p * far[0].shape[0]
                final = p + 1 == len(far_xs)
                state = front(ids, far, half, offset, tokens, wt, ft, update_mask, parts, state, final)
            q, k, v, *grads = state
            near = grads[0].astype(F32)
            for i in range(1, views // 2):
                part = swap(grads[i % heads], VIEW, 2 * i, lambda _, o: (o >> 1) < heads)
                near = near + part.astype(F32)
            near = near.astype(BF16)
            got = swap(near, VIEW, 1)
            count = half * tokens
            attended = None
            least = count // 2
            for start, n in ((least, 2 * count - least), (0, least)):
                attended = attend(q, k, v, start, n, attended)
            fresh = newton(ids, ft, near, got)
            fast = [fresh] + [swap(fresh, VIEW, 2 * i, lambda i, o: (i >> 1) < heads) for i in range(1, views // 2)]
            received, places = [], []
            far_chunks = [(c, 1) for c in range(half)]
            if staged:
                spans = [(0, half)] + [(c, 1) for c in range(half, parts)]
                early, *sent = apply_fast(ids, q, attended, fast, heads, EARLY, tokens, 0, spans)
                for i, x in enumerate(sent, half):
                    received.append(swap(x, HEAD, i))
                    places.append((i, 0))
                sent = apply_fast(ids, q, attended, fast, heads, LATE, tokens, half, far_chunks)
                for i, x in enumerate(sent, half):
                    received.append(swap(x, HEAD, i))
                    places.append((i, 1))
                mixed = apply_fast(ids, q, attended, fast, heads, LATE, tokens, 0, far_chunks, early)
            else:
                sent = apply_fast(ids, q, attended, fast, heads, ALL, tokens, half, far_chunks)
                for i, x in enumerate(sent, half):
                    received.append(swap(x, HEAD, i))
                    places.append((i, None))
                mixed = apply_fast(ids, q, attended, fast, heads, ALL, tokens, 0, far_chunks)
            near_parts = [x if i == 0 else swap(x, HEAD, i) for i, x in enumerate(mixed)]
            received = near_parts + received
            places = [(i, None) for i in range(half)] + places
            more = layer + 1 < blocks
            result = project(ids, stream, out_own, out_pair, layer, received, places, heads, dim, more)
            stream = result[0]
            if more:
                normed, *halves = result[1:]
        return stream


    return jax.shard_map(
        shards,
        mesh=mesh,
        in_specs=(
            P((VIEW, HEAD), None),
            P(None, None, VIEW, HEAD),
            P(None, VIEW, None),
            P(None, HEAD, None, None, VIEW),
            P(VIEW, None),
        ),
        out_specs=P((VIEW, HEAD), None),
        check_vma=False,
    )
```
